256 devices in a mesh: param: 16 (over x, y), slab: 16 (over z, core).
Axes of the slice: x: 4, y: 4, z: 8, core: 2. Of those that a mesh axis runs over, the one named last changes fastest.
Arguments:
- init_state: float32 [16, 128, 256, 128], P('param', None, 'slab'), may hold values from -6 to 6
- coef: float32 [16, 256, 128], P('param', 'slab'), may hold values from 0.06 to 0.16
- source: float32 [256, 128], P('slab'), may hold values from -6 to 6
- amplitudes: float32 [64], replicated, may hold values from 0.5 to 2
- sample_idx: int32 [16, 128], P('param'), may hold values from 0 to 63
- step_counts: int32 [16], P('param'), may hold values from 1 to 8, as said below
- sketch_signs: int32 [5, 128, 64], replicated, may hold values from 0 to 1
Outputs:
- modes: float32 [64, 256, 128], P(None, 'slab', 'param')
The draws below stay inside these ranges and needn't reach their ends.
Inputs may be any that keep to these rules, and one draw needn't show every extreme that they name: `step_counts`: one group takes all 8 steps and another exactly one.
All inputs are finite; a program needn't handle non-finite values.
Results may differ from the reference program's by a relative error of at most 0.0003.
Values sent between devices are 32-bit elements; how exact they have to be, the bound alone decides.
No kernel may reach another device: no remote copies, remote signals or barrier semaphores. Data moves between devices by JAX's collectives and lax.ppermute only.
A program may use at most 64 MiB of HBM per device.

```python
import math
import jax
import jax.numpy as jnp
from jax import lax

S = 128
R = 64
NZ = 128
STEPS = 8
PTAB = 64
GROUPS = 16
NX = 256
LEVELS = 4


def draw_step_counts(key, part):
    first_key, second_key = jax.random.split(jax.random.fold_in(key, 7))
    counts = jax.random.randint(first_key, (GROUPS,), 1, STEPS + 1)
    order = jax.random.permutation(second_key, GROUPS)
    counts = counts.at[order[0]].set(STEPS)
    counts = counts.at[order[1]].set(1)
    return counts.astype(jnp.int32)


def with_ends(entries, stream_key, smallest, top_value):
    extent = entries.shape
    index_at = [jax.random.randint(jax.random.fold_in(stream_key, axis), (), 0, extent[axis]) for axis in range(len(extent))]
    entries = entries.at[tuple(index_at)].set(smallest)
    longest = extent.index(max(extent))
    index_at[longest] = (index_at[longest] + 1) % extent[longest]
    return entries.at[tuple(index_at)].set(top_value)


def shard_levels(key, dims, shards, low, top_value):
    def one(axis_at, blocks):
        steps = jax.random.uniform(jax.random.fold_in(jax.random.fold_in(key, 6), axis_at), (blocks,), jnp.float32, low / len(shards), top_value / len(shards))
        return jnp.repeat(jnp.exp(steps), dims[axis_at] // blocks).reshape((-1,) + (1,) * (len(dims) - axis_at - 1))

    loudness = one(*shards[0])
    for cut in shards[1:]:
        loudness = loudness * one(*cut)
    return loudness


def normal_values(own_key, extent, deviation, bound, cuts=(), held_as=jnp.bfloat16):
    level = shard_levels(own_key, extent, cuts, -0.22, 0.18) if cuts else 1.0
    result = jax.random.normal(own_key, extent, jnp.float32) * deviation * level
    return jnp.minimum(jnp.maximum(result, -bound), bound).astype(held_as)


def setup_inputs(seed: int = 0) -> dict:
    key_list = jax.random.split(jax.random.key(seed), 8)
    return {
        "init_state": normal_values(key_list[0], (GROUPS, S, NX, NZ), 1.0, 6.0, ((0, 16), (2, 16)), jnp.float32),
        "coef": jnp.clip(jnp.exp(math.log(0.16) - 0.98082925 * jax.random.uniform(key_list[1], (GROUPS, NX, NZ), jnp.float32) ** shard_levels(key_list[1], (GROUPS, NX, NZ), ((0, 16), (1, 16)), -0.2, 0.2)), 0.06, 0.16),
        "source": normal_values(key_list[2], (NX, NZ), 1.0, 6.0, ((0, 16),), jnp.float32),
        "amplitudes": jnp.clip(jnp.exp(jax.random.uniform(key_list[3], (PTAB,), jnp.float32, math.log(0.5), math.log(2.0))), 0.5, 2.0),
        "sample_idx": with_ends(jax.random.randint(key_list[4], (GROUPS, S), 0, PTAB), jax.random.fold_in(key_list[4], 1), 0, PTAB - 1).astype(jnp.int32),
        "step_counts": draw_step_counts(jax.random.fold_in(key_list[7], 71), 0),
        "sketch_signs": with_ends(jax.random.randint(key_list[6], (LEVELS + 1, S, R), 0, 2), jax.random.fold_in(key_list[6], 1), 0, 1).astype(jnp.int32),
    }


def omega_rows(sketch_signs, level):
    signs = sketch_signs[level].astype(jnp.float32)
    return (2.0 * signs - 1.0).T / math.sqrt(sketch_signs.shape[1])

def compress(stacked, gram, omega_t):
    highest = lax.Precision.HIGHEST
    modes_kept = omega_t.shape[0]
    ident = jnp.eye(modes_kept, dtype=jnp.float32)
    moment = jnp.dot(jnp.dot(omega_t, gram, precision=highest), omega_t.T, precision=highest)
    moment = moment + 0.0001 * jnp.trace(moment) / modes_kept * ident
    lower = jnp.linalg.cholesky(moment)
    left = jax.scipy.linalg.solve_triangular(lower, omega_t, lower=True)
    hmat = jnp.dot(left, gram, precision=highest)
    inner = jnp.dot(hmat, hmat.T, precision=highest)
    inner = inner + 0.0001 * jnp.trace(inner) / modes_kept * ident
    factor = jnp.linalg.cholesky(inner)
    mixing = jnp.dot(factor.T, left, precision=highest)
    return jnp.dot(mixing, stacked, precision=highest)

def reference(init_state, coef, source, amplitudes, sample_idx, step_counts, sketch_signs):
    highest = lax.Precision.HIGHEST

    def leaf(inputs):
        field, rate_base, picks, count = inputs
        amp = amplitudes[picks]
        forcing = 0.1 * amp[:, None, None] * source[None]
        for step in range(STEPS):
            padded = jnp.pad(field, ((0, 0), (1, 1), (1, 1)))
            lap = padded[:, 2:, 1:-1] + padded[:, :-2, 1:-1] + padded[:, 1:-1, 2:] + padded[:, 1:-1, :-2] - 4.0 * field
            new = field + rate_base * (1.0 + 0.5 * jnp.tanh(field) ** 2) * lap + forcing
            field = jnp.where(step < count, new, field)
        stacked = field.reshape(field.shape[0], -1)
        gram = jnp.dot(stacked, stacked.T, precision=highest)
        return compress(stacked, gram, omega_rows(sketch_signs, 0))
    pieces = lax.map(leaf, (init_state, coef, sample_idx, step_counts))
    scale_half = 0.5 ** 0.5
    for level in range(LEVELS):
        paired = pieces.reshape(pieces.shape[0] // 2, 2 * pieces.shape[1], pieces.shape[2])
        omega_t = omega_rows(sketch_signs, level + 1)

        def merge(stacked):
            stacked = stacked * scale_half
            gram = jnp.dot(stacked, stacked.T, precision=highest)
            return compress(stacked, gram, omega_t)
        pieces = lax.map(merge, paired)
    return pieces[0].reshape(pieces.shape[1], NX, NZ)
```

```python
import functools
import math

import jax
import jax.numpy as jnp
from jax import lax
from jax.experimental import pallas as pl
from jax.experimental.pallas import tpu as pltpu
from jax.sharding import Mesh
from jax.sharding import PartitionSpec as P

STEPS = 8
HI = lax.Precision.HIGHEST
F32 = jnp.float32
VMEM = pl.BlockSpec(memory_space=pltpu.VMEM)
SMEM = pl.BlockSpec(memory_space=pltpu.SMEM)


def mm(a, b):
    return lax.dot_general(
        a, b, (((1,), (0,)), ((), ())), precision=HI, preferred_element_type=F32
    )


def mm_nt(a, b):
    return lax.dot_general(
        a, b, (((1,), (1,)), ((), ())), precision=HI, preferred_element_type=F32
    )


def lanes_of(v, k):
    return jnp.broadcast_to(v[:, k : k + 1], v.shape)


def rows_of(v, i):
    return jnp.broadcast_to(v[i : i + 1, :], v.shape)


def factor(blocks):
    work = list(blocks)
    sub = lax.broadcasted_iota(jnp.int32, work[0].shape, 0)
    done = []
    for kb in range(8):
        k = 8 * kb
        cols = [[lanes_of(work[i], k + j) for i in range(kb, 8)] for j in range(8)]
        rows = [rows_of(work[kb], j) for j in range(8)]
        el = [[rows_of(cols[j][0], i) if i <= j else None for j in range(8)] for i in range(8)]
        scaled = []
        for p in range(8):
            inv = 1.0 / el[p][p]
            scaled.append(rows[p] * inv)
            mult = [el[p][j] * inv if j > p else None for j in range(8)]
            for j in range(p + 1, 8):
                for i in range(p + 1, j + 1):
                    el[i][j] = el[i][j] - mult[i] * el[p][j]
            for j in range(p + 1, 8):
                rows[j] = rows[j] - mult[j] * rows[p]
                for n in range(1, 8 - kb):
                    cols[j][n] = cols[j][n] - cols[p][n] * mult[j]
        out = rows[0] * lax.rsqrt(el[0][0])
        for p in range(1, 8):
            out = jnp.where(sub == p, rows[p] * lax.rsqrt(el[p][p]), out)
        done.append(out)
        for i in range(kb + 1, 8):
            for p in range(8):
                work[i] = work[i] - cols[p][i - kb] * scaled[p]
    return jnp.concatenate(done, axis=0)


def shifted(mat, extra):
    row = lax.broadcasted_iota(jnp.int32, mat.shape, 0)
    lane = lax.broadcasted_iota(jnp.int32, mat.shape, 1)
    diag = lane == row
    trace = jnp.sum(jnp.where(diag, mat, 0.0), keepdims=True)
    mat = mat + jnp.where(diag, trace * (0.0001 / 64.0), 0.0)
    if extra:
        mat = jnp.where(lane == row + 64, 1.0, mat)
    return [mat[8 * i : 8 * i + 8] for i in range(8)]


def compress_all(yts, om_pad):
    moments = [mm(yt, om_pad) for yt in yts]
    firsts = [factor(shifted(m, True)) for m in moments]
    linvs = [f[:, 64:] for f in firsts]
    hs = [mm(li, yt) for li, yt in zip(linvs, yts)]
    pad = jnp.zeros((64, 128), F32)
    inners = [mm_nt(h, jnp.concatenate([h, pad], axis=0)) for h in hs]
    seconds = [factor(shifted(c, False)) for c in inners]
    row = lax.broadcasted_iota(jnp.int32, (64, 64), 0)
    lane = lax.broadcasted_iota(jnp.int32, (64, 64), 1)
    kts = [jnp.where(lane >= row, s[:, :64], 0.0) for s in seconds]
    return [mm(k, li) for k, li in zip(kts, linvs)], [m[:, :64] for m in moments]


def omega_of(signs_ref, level):
    signs = signs_ref[level].astype(F32)
    om = (2.0 * signs - 1.0) * (1.0 / math.sqrt(128.0))
    return jnp.concatenate([om, jnp.zeros((128, 64), F32)], axis=1)


def both_halves(core, own_ref, other_ref):
    own = own_ref[...]
    other = other_ref[...]
    first = core == 0
    return jnp.concatenate(
        [jnp.where(first, own, other), jnp.where(first, other, own)], axis=0
    )


def exchange_blocks(vals, bit, lane_bit):
    lane = lax.broadcasted_iota(jnp.int32, vals[0].shape, 1)
    low = (lane & lane_bit) == 0
    out = list(vals)
    for i in range(len(vals)):
        if i & bit:
            continue
        a, b = vals[i], vals[i | bit]
        out[i] = jnp.where(low, a, pltpu.roll(b, lane_bit, 1))
        out[i | bit] = jnp.where(low, pltpu.roll(a, 128 - lane_bit, 1), b)
    return out


def flow_kernel(
    count_ref, x_ref, bef_ref, aft_ref, rate_ref, src_ref, amp_ref, signs_ref,
    s_ref, yt_ref, c_s, h_s, src_s, f_s, field_s,
):
    for r in range(32):
        if r < 8:
            rate, src = bef_ref[1024 + r : 1025 + r, :], bef_ref[1032 + r : 1033 + r, :]
        elif r < 24:
            rate, src = rate_ref[r - 8 : r - 7, :], src_ref[r - 8 : r - 7, :]
        else:
            rate, src = aft_ref[1000 + r : 1001 + r, :], aft_ref[1008 + r : 1009 + r, :]
        at = slice(8 * r, 8 * r + 8)
        c_s[at, :] = jnp.broadcast_to(rate, (8, 128))
        h_s[at, :] = jnp.broadcast_to(0.5 * rate, (8, 128))
        src_s[at, :] = jnp.broadcast_to(src, (8, 128))
    count = count_ref[0]
    lane = lax.broadcasted_iota(jnp.int32, (8, 128), 1)
    not_first = lane != 0
    not_last = lane != 127

    def block(b, carry):
        amp = amp_ref[pl.ds(pl.multiple_of(b * 8, 8), 8), :]
        old = []
        for r in range(32):
            if r < 8:
                old.append(bef_ref[pl.ds(b * 64 + r, 8, stride=8), :])
            elif r < 24:
                old.append(x_ref[pl.ds(b * 128 + (r - 8), 8, stride=16), :])
            else:
                old.append(aft_ref[pl.ds(b * 64 + (r - 24), 8, stride=8), :])
            f_s[8 * r : 8 * r + 8, :] = amp * src_s[8 * r : 8 * r + 8, :]
        for t in range(STEPS):
            live = t < count
            new = list(old)
            for r in range(t + 1, 31 - t):
                at = slice(8 * r, 8 * r + 8)
                mid = old[r]
                left = jnp.where(not_first, pltpu.roll(mid, 1, 1), 0.0)
                right = jnp.where(not_last, pltpu.roll(mid, 127, 1), 0.0)
                lap = (old[r + 1] + old[r - 1]) + (right + left) - 4.0 * mid
                bend = jnp.tanh(mid)
                val = mid + (c_s[at, :] + h_s[at, :] * (bend * bend)) * lap + f_s[at, :]
                new[r] = jnp.where(live, val, mid)
            old = new
        for r in range(16):
            field_s[r, pl.ds(pl.multiple_of(b * 8, 8), 8), :] = old[8 + r]
        return carry

    lax.fori_loop(0, 16, block, 0)
    om_t = omega_of(signs_ref, 0).T[:64]
    yt = jnp.zeros((64, 128), F32)
    for q in range(4):
        parts = []
        for i in range(4):
            own = field_s[4 * q + i]
            sk = mm(om_t, own)
            yt = yt + mm_nt(sk, own)
            parts.append(sk)
        parts = exchange_blocks(exchange_blocks(parts, 1, 8), 2, 16)
        for j in range(4):
            s_ref[j, q] = parts[j]
    yt_ref[...] = yt


def leaf_kernel(pos_ref, own_ref, other_ref, s_ref, signs_ref, d0, d1, d2, d3):
    yt = both_halves(pos_ref[0], own_ref, other_ref)
    (b,), _ = compress_all([yt], omega_of(signs_ref, 0))
    place = pos_ref[1]
    for d, out in enumerate((d0, d1, d2, d3)):
        part = s_ref[lax.rem(place + d, 4)]
        for q in range(4):
            out[q] = mm(b, part[q])


def sketch_kernel(level, pos_ref, r0, r1, r2, r3, signs_ref, s_ref, pay_ref, all_s):
    place = pos_ref[0]
    for d, ref in enumerate((r0, r1, r2, r3)):
        all_s[lax.rem(place + (4 - d), 4)] = ref[...] * (0.5**0.5)
    om_t = omega_of(signs_ref, level).T[:64]
    yts = [jnp.zeros((64, 128), F32)] * 2
    cross = jnp.zeros((64, 64), F32)
    for q in range(4):
        sks = []
        for n in range(2):
            own = jnp.concatenate([all_s[2 * n, q], all_s[2 * n + 1, q]], axis=0)
            sk = mm(om_t, own)
            yts[n] = yts[n] + mm_nt(sk, own)
            s_ref[n, q] = sk
            sks.append(sk)
        cross = cross + mm_nt(sks[0], sks[1])
    pay_ref[0:64] = yts[0]
    pay_ref[64:128] = yts[1]
    pay_ref[128:160] = jnp.concatenate([cross[:32], cross[32:]], axis=1)


def two_levels(level, core, own_ref, other_ref, signs_ref, bd_s, n_s):
    pay = both_halves(core, own_ref, other_ref)
    yts = [pay[:64], pay[64:128]]
    cross = jnp.concatenate([pay[128:160, :64], pay[128:160, 64:]], axis=0)
    bs, moments = compress_all(yts, omega_of(signs_ref, level))
    zero = jnp.zeros((64, 64), F32)
    bd_s[0:64] = jnp.concatenate([bs[0], zero], axis=1)
    bd_s[64:128] = jnp.concatenate([zero, bs[1]], axis=1)
    n_s[0:64] = jnp.concatenate([moments[0], cross], axis=1)
    n_s[64:128] = jnp.concatenate([cross.T, moments[1]], axis=1)
    om_pad = omega_of(signs_ref, level + 1)
    v = mm(om_pad.T[:64], bd_s[...])
    yt = 0.5 * mm_nt(mm(v, n_s[...]), bd_s[...])
    (b,), _ = compress_all([yt], om_pad)
    return mm(b, v) * (0.5**0.5)


def middle_kernel(level, pos_ref, own_ref, other_ref, s_ref, signs_ref, out_ref, bd_s, n_s):
    w = two_levels(level, pos_ref[0], own_ref, other_ref, signs_ref, bd_s, n_s)
    for q in range(4):
        out_ref[q] = mm(w, jnp.concatenate([s_ref[0, q], s_ref[1, q]], axis=0))


def last_kernel(level, pos_ref, own_ref, other_ref, s_ref, signs_ref, out_ref, bd_s, n_s):
    w = two_levels(level, pos_ref[0], own_ref, other_ref, signs_ref, bd_s, n_s)
    place = pos_ref[1]
    lane = lax.broadcasted_iota(jnp.int32, (128, 128), 1)
    block = lax.shift_right_logical(lane, 5)
    mine = jnp.zeros((128, 128), F32)
    for q in range(4):
        own = jnp.concatenate([s_ref[0, q], s_ref[1, q]], axis=0)
        turned = pltpu.roll(own, lax.rem(32 * q - 32 * place + 128, 128), 1)
        mine = jnp.where(block == q, turned, mine)
    out_ref[...] = mm(w, mine)


def call(kernel, out_shapes, smem, *args, scratch=()):
    specs = [SMEM] * smem + [VMEM] * (len(args) - smem)
    return pl.pallas_call(
        kernel,
        out_shape=out_shapes,
        in_specs=specs,
        out_specs=jax.tree.map(lambda _: VMEM, out_shapes),
        scratch_shapes=list(scratch),
    )(*args)


def shape(*dims):
    return jax.ShapeDtypeStruct(dims, F32)


def shift(value, axis, by):
    n = lax.axis_size(axis)
    return lax.ppermute(value, axis, [(i, (i + by) % n) for i in range(n)])


def half_over_cores(value, core):
    rows = value.shape[0] // 2
    total = value + shift(value, "core", 1)
    return lax.dynamic_slice_in_dim(total, core * rows, rows, 0)


def sum_over(value, axis):
    peers = lax.axis_size(axis)
    sent = jnp.broadcast_to(value[None], (peers, *value.shape))
    return lax.all_to_all(sent, axis, 0, 0, tiled=True).sum(axis=0)


def sum_over_ring(value, axis):
    parts = [value] + [shift(value, axis, d) for d in (1, 2, 3)]
    return (parts[0] + parts[1]) + (parts[2] + parts[3])


def per_device(init_state, coef, source, amplitudes, sample_idx, step_counts, sketch_signs):
    field = init_state[0]
    rate = coef[0]
    core = lax.axis_index("core")
    xi = lax.axis_index("x")
    yi = lax.axis_index("y")
    table = amplitudes.shape[0]
    picks = sample_idx[0][:, None] == jnp.arange(table, dtype=jnp.int32)[None, :]
    amp = 0.1 * jnp.sum(jnp.where(picks, amplitudes[None, :], 0.0), axis=1)
    amp = jnp.broadcast_to(amp[:, None], (128, 128))

    slabs = ("z", "core")
    n = lax.axis_size(slabs)
    up = [(i, i + 1) for i in range(n - 1)]
    down = [(i + 1, i) for i in range(n - 1)]
    tail = jnp.concatenate([field[:, 8:], rate[None, 8:], source[None, 8:]], axis=0)
    head = jnp.concatenate([field[:, :8], rate[None, :8], source[None, :8]], axis=0)
    bef = lax.ppermute(tail, slabs, up)
    aft = lax.ppermute(head, slabs, down)

    s0, yt0 = call(
        flow_kernel,
        (shape(4, 4, 64, 128), shape(64, 128)),
        1,
        step_counts,
        field.reshape(2048, 128),
        bef.reshape(1040, 128),
        aft.reshape(1040, 128),
        rate,
        source,
        amp,
        sketch_signs,
        scratch=[pltpu.VMEM((256, 128), F32)] * 4 + [pltpu.VMEM((16, 128, 128), F32)],
    )
    own = sum_over(half_over_cores(yt0, core), "z")
    other = shift(own, "core", 1)
    pieces = call(
        leaf_kernel,
        (shape(4, 64, 128),) * 4,
        1,
        jnp.stack([core, yi]).astype(jnp.int32),
        own,
        other,
        s0,
        sketch_signs,
    )
    for level, axis, place in ((1, "y", yi), (3, "x", xi)):
        if level == 1:
            got = [pieces[0]] + [shift(pieces[d], axis, d) for d in (1, 2, 3)]
        else:
            got = [pieces] + [shift(pieces, axis, d) for d in (1, 2, 3)]
        s, pay = call(
            functools.partial(sketch_kernel, level),
            (shape(2, 4, 64, 128), shape(160, 128)),
            1,
            place.astype(jnp.int32)[None],
            *got,
            sketch_signs,
            scratch=[pltpu.VMEM((4, 4, 64, 128), F32)],
        )
        own = sum_over(sum_over_ring(half_over_cores(pay, core), "y"), "z")
        other = shift(own, "core", 1)
        scratch = [pltpu.VMEM((128, 128), F32)] * 2
        pieces = call(
            functools.partial(middle_kernel if level == 1 else last_kernel, level),
            shape(4, 64, 128) if level == 1 else shape(64, 128),
            1,
            jnp.stack([core, xi]).astype(jnp.int32),
            own,
            other,
            s,
            sketch_signs,
            scratch=scratch,
        )
    return pieces.reshape(64, 16, 8)


def solution(mesh):
    fine = Mesh(mesh.devices.reshape(4, 4, 8, 2), ("x", "y", "z", "core"))
    group, slab = ("x", "y"), ("z", "core")
    return jax.shard_map(
        per_device,
        mesh=fine,
        in_specs=(
            P(group, None, slab, None),
            P(group, slab, None),
            P(slab, None),
            P(),
            P(group, None),
            P(group),
            P(),
        ),
        out_specs=P(None, slab, group),
        check_vma=False,
    )
```

```python
import functools
import math

import jax
import jax.numpy as jnp
from jax import lax
from jax.experimental import pallas as pl
from jax.experimental.pallas import tpu as pltpu
from jax.sharding import Mesh
from jax.sharding import PartitionSpec as P

STEPS = 8
SCALE = 1.0 / math.sqrt(128.0)
HI = lax.Precision.HIGHEST
F32 = jnp.float32
VMEM = pl.BlockSpec(memory_space=pltpu.VMEM)
SMEM = pl.BlockSpec(memory_space=pltpu.SMEM)


def mm(a, b):
    return lax.dot_general(
        a, b, (((1,), (0,)), ((), ())), precision=HI, preferred_element_type=F32
    )


def mm_nt(a, b):
    return lax.dot_general(
        a, b, (((1,), (1,)), ((), ())), precision=HI, preferred_element_type=F32
    )


def thirds(x):
    hi = x.astype(jnp.bfloat16)
    rest = x - hi.astype(F32)
    mid = rest.astype(jnp.bfloat16)
    return hi, mid, (rest - mid.astype(F32)).astype(jnp.bfloat16)


def signs_mm(signs, x):
    hi, mid, lo = (jnp.dot(signs, t, preferred_element_type=F32) for t in thirds(x))
    return (hi + (mid + lo)) * SCALE


def mm_signs(x, signs):
    hi, mid, lo = (jnp.dot(t, signs, preferred_element_type=F32) for t in thirds(x))
    return (hi + (mid + lo)) * SCALE


def rows_of(v, i):
    return jnp.broadcast_to(v[i : i + 1, :], v.shape)


def factor(blocks, split):
    work = list(blocks)
    shape_of = work[0].shape
    sub = lax.broadcasted_iota(jnp.int32, shape_of, 0)
    lane = lax.broadcasted_iota(jnp.int32, shape_of, 1)
    base = jnp.where(lane < 64, 0, 64) if split else jnp.zeros(shape_of, jnp.int32)
    done = []
    for kb in range(8):
        cols = []
        for j in range(8):
            index = base + (8 * kb + j)
            cols.append([jnp.take_along_axis(work[i], index, axis=1) for i in range(kb, 8)])
        rows = [rows_of(work[kb], j) for j in range(8)]
        el = [[rows_of(cols[j][0], i) if i <= j else None for j in range(8)] for i in range(8)]
        outs, scaled = [], []
        for p in range(0, 8, 2):
            q = p + 1
            a, b, c = el[p][p], el[p][q], el[q][q]
            det = a * c - b * b
            inv = 1.0 / det
            rp, rq = rows[p], rows[q]
            root = lax.rsqrt(a)
            outs += [rp * root, (a * rq - b * rp) * (root * lax.rsqrt(det))]
            off = b * inv
            scaled += [(c * inv) * rp - off * rq, (a * inv) * rq - off * rp]
            left = {j: c * el[p][j] - b * el[q][j] for j in range(q + 1, 8)}
            right = {j: a * el[q][j] - b * el[p][j] for j in range(q + 1, 8)}
            for j in range(q + 1, 8):
                x, y = left[j] * inv, right[j] * inv
                for i in range(q + 1, j + 1):
                    el[i][j] = el[i][j] - (el[p][i] * left[j] + el[q][i] * right[j]) * inv
                rows[j] = rows[j] - (x * rp + y * rq)
                for n in range(1, 8 - kb):
                    cols[j][n] = cols[j][n] - (cols[p][n] * x + cols[q][n] * y)
        out = outs[0]
        for p in range(1, 8):
            out = jnp.where(sub == p, outs[p], out)
        done.append(out)
        for i in range(kb + 1, 8):
            acc = [cols[p][i - kb] * scaled[p] for p in range(8)]
            while len(acc) > 1:
                acc = [acc[2 * t] + acc[2 * t + 1] for t in range(len(acc) // 2)]
            work[i] = work[i] - acc[0]
    return jnp.concatenate(done, axis=0)


def shift_of(mat, diag):
    trace = jnp.sum(jnp.where(diag, mat, 0.0), keepdims=True)
    return jnp.where(diag, trace * (0.0001 / 64.0), 0.0)


def row_blocks(mat):
    return [mat[8 * i : 8 * i + 8] for i in range(8)]


def compress(yts, signs):
    row = lax.broadcasted_iota(jnp.int32, (64, 128), 0)
    lane = lax.broadcasted_iota(jnp.int32, (64, 128), 1)
    diag = lane == row
    wide = jnp.concatenate([signs, jnp.zeros((128, 64), jnp.bfloat16)], axis=1)
    moments = [mm_signs(yt, wide) for yt in yts]
    firsts = [
        factor(row_blocks(jnp.where(lane == row + 64, 1.0, m + shift_of(m, diag))), False)
        for m in moments
    ]
    linvs = [f[:, 64:] for f in firsts]
    hs = [mm(li, yt) for li, yt in zip(linvs, yts)]
    if len(hs) == 1:
        pad = jnp.zeros((64, 128), F32)
        inner = mm_nt(hs[0], jnp.concatenate([hs[0], pad], axis=0))
        inner = inner + shift_of(inner, diag)
        second = factor(row_blocks(inner), False)
        kts = [jnp.where(lane >= row, second, 0.0)[:, :64]]
    else:
        small = [mm_nt(h, h) for h in hs]
        small = [c + shift_of(c, diag[:, :64]) for c in small]
        second = factor(row_blocks(jnp.concatenate(small, axis=1)), True)
        second = jnp.where((lane & 63) >= row, second, 0.0)
        kts = [second[:, :64], second[:, 64:]]
    return [mm(k, li) for k, li in zip(kts, linvs)], [m[:, :64] for m in moments]


def gram_of(b, moment):
    return mm_nt(mm(b, moment), b)


def sketch_of_pair(first, cross, second, signs_t):
    top = jnp.concatenate([first, cross], axis=1)
    bottom = jnp.concatenate([cross.T, second], axis=1)
    return 0.5 * signs_mm(signs_t, jnp.concatenate([top, bottom], axis=0))


def signs_of(signs_ref, level):
    signs = 2.0 * signs_ref[level].astype(F32) - 1.0
    return signs.astype(jnp.bfloat16), signs.T.astype(jnp.bfloat16)


def both_halves(own_ref, other_ref):
    first = lax.axis_index("core") == 0
    own = own_ref[...]
    other = other_ref[...]
    return jnp.where(first, own, other), jnp.where(first, other, own)


def rest_of(value, by):
    return lax.rem(value + (by + 4), 4)


def exchange_blocks(vals, bit, lane_bit):
    lane = lax.broadcasted_iota(jnp.int32, vals[0].shape, 1)
    low = (lane & lane_bit) == 0
    out = list(vals)
    for i in range(len(vals)):
        if i & bit:
            continue
        a, b = vals[i], vals[i | bit]
        out[i] = jnp.where(low, a, pltpu.roll(b, lane_bit, 1))
        out[i | bit] = jnp.where(low, pltpu.roll(a, 128 - lane_bit, 1), b)
    return out


def flow_kernel(
    count_ref, x_ref, bef_ref, aft_ref, rate_ref, src_ref, amp_ref, signs_ref,
    yt_ref, d0, d1, d2, d3, c_s, h_s, src_s, f_s, field_s, s_s,
):
    for r in range(32):
        if r < 8:
            rate, src = bef_ref[1024 + r : 1025 + r, :], bef_ref[1032 + r : 1033 + r, :]
        elif r < 24:
            rate, src = rate_ref[r - 8 : r - 7, :], src_ref[r - 8 : r - 7, :]
        else:
            rate, src = aft_ref[1000 + r : 1001 + r, :], aft_ref[1008 + r : 1009 + r, :]
        at = slice(8 * r, 8 * r + 8)
        c_s[at, :] = jnp.broadcast_to(rate, (8, 128))
        h_s[at, :] = jnp.broadcast_to(0.5 * rate, (8, 128))
        src_s[at, :] = jnp.broadcast_to(src, (8, 128))
    count = count_ref[0]
    lane = lax.broadcasted_iota(jnp.int32, (8, 128), 1)
    not_first = lane != 0
    not_last = lane != 127

    def block(b, carry):
        amp = amp_ref[pl.ds(pl.multiple_of(b * 8, 8), 8), :]
        old = []
        for r in range(32):
            if r < 8:
                old.append(bef_ref[pl.ds(b * 64 + r, 8, stride=8), :])
            elif r < 24:
                old.append(x_ref[pl.ds(b * 128 + (r - 8), 8, stride=16), :])
            else:
                old.append(aft_ref[pl.ds(b * 64 + (r - 24), 8, stride=8), :])
            f_s[8 * r : 8 * r + 8, :] = amp * src_s[8 * r : 8 * r + 8, :]
        for t in range(STEPS):
            live = t < count
            new = list(old)
            for r in range(t + 1, 31 - t):
                at = slice(8 * r, 8 * r + 8)
                mid = old[r]
                left = jnp.where(not_first, pltpu.roll(mid, 1, 1), 0.0)
                right = jnp.where(not_last, pltpu.roll(mid, 127, 1), 0.0)
                lap = (old[r + 1] + old[r - 1]) + (right + left) - 4.0 * mid
                bend = jnp.tanh(mid)
                val = mid + (c_s[at, :] + h_s[at, :] * (bend * bend)) * lap + f_s[at, :]
                new[r] = jnp.where(live, val, mid)
            old = new
        for r in range(16):
            field_s[r, pl.ds(pl.multiple_of(b * 8, 8), 8), :] = old[8 + r]
        return carry

    lax.fori_loop(0, 16, block, 0)
    _, signs_t = signs_of(signs_ref, 0)
    yt = jnp.zeros((64, 128), F32)
    for q in range(4):
        parts = []
        for i in range(4):
            own = field_s[4 * q + i]
            sk = signs_mm(signs_t, own)
            yt = yt + mm_nt(sk, own)
            parts.append(sk)
        parts = exchange_blocks(exchange_blocks(parts, 1, 8), 2, 16)
        for j in range(4):
            s_s[j, q] = parts[j]
    yt_ref[...] = yt
    place = lax.axis_index("y")
    for d, out in enumerate((d0, d1, d2, d3)):
        out[...] = s_s[rest_of(place, d)]


def cross_kernel(yt_ref, r0, r1, r2, r3, keep_ref, send_ref, all_s, z_s, pay_s):
    place = lax.axis_index("y")
    for d, ref in enumerate((r0, r1, r2, r3)):
        all_s[rest_of(place, -d)] = ref[...]
    slabs = [jnp.zeros((64, 128), F32)] * 3
    for q in range(4):
        s0, s1, s2, s3 = (all_s[g, q] for g in range(4))
        upper = jnp.concatenate([s2, s3], axis=0)
        first = mm_nt(s0, jnp.concatenate([s1, s3], axis=0))
        slabs[1] = slabs[1] + mm_nt(s0, upper)
        slabs[2] = slabs[2] + mm_nt(s1, upper)
        slabs[0] = slabs[0] + jnp.concatenate([first[:, :64], mm_nt(s2, s3)], axis=1)
    for n in range(3):
        z_s[64 * n : 64 * n + 64] = slabs[n]
    for c in range(2):
        pay_s[c, 0:32] = yt_ref[32 * c : 32 * c + 32]
        for d in range(4):
            at = pl.multiple_of(48 * rest_of(place, d) + 24 * c, 8)
            pay_s[c, 32 + 24 * d : 56 + 24 * d] = z_s[pl.ds(at, 24), :]
    core = lax.axis_index("core")
    keep_ref[...] = pay_s[core]
    send_ref[...] = pay_s[1 - core]


def leaf_kernel(own_ref, other_ref, signs_ref, out_ref):
    low, high = both_halves(own_ref, other_ref)
    signs, _ = signs_of(signs_ref, 0)
    (b,), (moment,) = compress([jnp.concatenate([low[:32], high[:32]], axis=0)], signs)
    out_ref[0:64] = jnp.concatenate([b, gram_of(b, moment)], axis=1)
    out_ref[64:88] = low[32:]
    out_ref[88:112] = high[32:]


def middle_kernel(p0, p1, p2, p3, all_ref, signs_ref, out_ref, pay_s, z_s):
    place = lax.axis_index("y")
    for d, ref in enumerate((p0, p1, p2, p3)):
        pay_s[rest_of(place, -d)] = ref[...]
    for g in range(4):
        z_s[48 * g : 48 * g + 48] = pay_s[g, 64:112]
    bs = [pay_s[g, 0:64][:, :64] for g in range(4)]
    grams = [pay_s[g, 0:64][:, 64:] for g in range(4)]
    inside = z_s[0:64]
    crosses = [mm_nt(mm(bs[0], inside[:, :64]), bs[1]), mm_nt(mm(bs[2], inside[:, 64:]), bs[3])]
    signs, signs_t = signs_of(signs_ref, 1)
    yts = [
        sketch_of_pair(grams[2 * n], crosses[n], grams[2 * n + 1], signs_t) for n in range(2)
    ]
    ups, moments = compress(yts, signs)
    half = 0.5**0.5
    ws = []
    for n in range(2):
        low = signs_mm(signs_t[:, :64], bs[2 * n])
        high = signs_mm(signs_t[:, 64:], bs[2 * n + 1])
        ws.append(mm(ups[n], jnp.concatenate([low, high], axis=1)) * half)
    cross = mm_nt(mm(ws[0], z_s[64:192]), ws[1])
    signs, signs_t = signs_of(signs_ref, 2)
    first, second = (gram_of(u, m) for u, m in zip(ups, moments))
    (b,), (moment,) = compress([sketch_of_pair(first, cross, second, signs_t)], signs)
    low = signs_mm(signs_t[:, :64], ws[0])
    high = signs_mm(signs_t[:, 64:], ws[1])
    w = mm(b, jnp.concatenate([low, high], axis=1)) * half
    for q in range(4):
        out_ref[64 * q : 64 * q + 64] = mm(
            w, jnp.concatenate([all_ref[g, q] for g in range(4)], axis=0)
        )
    gram = gram_of(b, moment)
    out_ref[256:288] = jnp.concatenate([gram[:32], gram[32:]], axis=1)


def upper_kernel(r0, r1, r2, r3, signs_ref, s_ref, keep_ref, send_ref, all_s, pay_s):
    place = lax.axis_index("x")
    for d, ref in enumerate((r0, r1, r2, r3)):
        all_s[rest_of(place, -d)] = ref[0:256]
    _, signs_t = signs_of(signs_ref, 3)
    slabs = [jnp.zeros((64, 64), F32)] * 3
    for q in range(4):
        at = slice(64 * q, 64 * q + 64)
        sks = []
        for n in range(2):
            low, high = all_s[2 * n, at], all_s[2 * n + 1, at]
            sk = signs_mm(signs_t, jnp.concatenate([low, high], axis=0)) * (0.5**0.5)
            s_ref[n, q] = sk
            sks.append(sk)
            slabs[n] = slabs[n] + mm_nt(low, high)
        slabs[2] = slabs[2] + mm_nt(*sks)
    for c in range(2):
        at = slice(32 * c, 32 * c + 32)
        pay_s[c, 0:32] = jnp.concatenate([slabs[0][at], slabs[1][at]], axis=1)
        pay_s[c, 32:48] = jnp.concatenate(
            [slabs[2][32 * c : 32 * c + 16], slabs[2][32 * c + 16 : 32 * c + 32]], axis=1
        )
    core = lax.axis_index("core")
    keep_ref[...] = pay_s[core]
    send_ref[...] = pay_s[1 - core]


def last_kernel(own_ref, other_ref, r0, r1, r2, r3, s_ref, signs_ref, out_ref, gram_s):
    place = lax.axis_index("x")
    for d, ref in enumerate((r0, r1, r2, r3)):
        gram_s[rest_of(place, -d)] = ref[256:288]
    grams = []
    for g in range(4):
        packed = gram_s[g]
        grams.append(jnp.concatenate([packed[:, :64], packed[:, 64:]], axis=0))
    low, high = both_halves(own_ref, other_ref)
    pairs = jnp.concatenate([low[:32], high[:32]], axis=0)
    inside = jnp.concatenate(
        [low[32:, :64], low[32:, 64:], high[32:, :64], high[32:, 64:]], axis=0
    )
    signs, signs_t = signs_of(signs_ref, 3)
    yts = [
        sketch_of_pair(grams[2 * n], pairs[:, 64 * n : 64 * n + 64], grams[2 * n + 1], signs_t)
        for n in range(2)
    ]
    bs, moments = compress(yts, signs)
    cross = mm_nt(mm(bs[0], inside), bs[1])
    first, second = (gram_of(u, m) for u, m in zip(bs, moments))
    signs, signs_t = signs_of(signs_ref, 4)
    (b,), _ = compress([sketch_of_pair(first, cross, second, signs_t)], signs)
    lower = signs_mm(signs_t[:, :64], bs[0])
    upper = signs_mm(signs_t[:, 64:], bs[1])
    w = mm(b, jnp.concatenate([lower, upper], axis=1)) * (0.5**0.5)
    lane = lax.broadcasted_iota(jnp.int32, (128, 128), 1)
    block = lax.shift_right_logical(lane, 5)
    mine = jnp.zeros((128, 128), F32)
    for q in range(4):
        own = jnp.concatenate([s_ref[0, q], s_ref[1, q]], axis=0)
        turned = pltpu.roll(own, lax.rem(32 * q - 32 * place + 128, 128), 1)
        mine = jnp.where(block == q, turned, mine)
    out_ref[...] = mm(w, mine)


def call(kernel, out_shapes, smem, *args, scratch=()):
    specs = [SMEM] * smem + [VMEM] * (len(args) - smem)
    return pl.pallas_call(
        kernel,
        out_shape=out_shapes,
        in_specs=specs,
        out_specs=jax.tree.map(lambda _: VMEM, out_shapes),
        scratch_shapes=list(scratch),
    )(*args)


def shape(*dims):
    return jax.ShapeDtypeStruct(dims, F32)


def shift(value, axis, by):
    n = lax.axis_size(axis)
    return lax.ppermute(value, axis, [(i, (i + by) % n) for i in range(n)])


def from_ring(value, axis):
    return [value] + [shift(value, axis, d) for d in (1, 2, 3)]


def total(parts):
    return (parts[0] + parts[1]) + (parts[2] + parts[3])


def sum_over(value, axis):
    peers = lax.axis_size(axis)
    sent = jnp.broadcast_to(value[None], (peers, *value.shape))
    return lax.all_to_all(sent, axis, 0, 0, tiled=True).sum(axis=0)


def per_device(init_state, coef, source, amplitudes, sample_idx, step_counts, sketch_signs):
    field = init_state[0]
    rate = coef[0]
    table = amplitudes.shape[0]
    picks = sample_idx[0][:, None] == jnp.arange(table, dtype=jnp.int32)[None, :]
    amp = 0.1 * jnp.sum(jnp.where(picks, amplitudes[None, :], 0.0), axis=1)
    amp = jnp.broadcast_to(amp[:, None], (128, 128))

    slabs = ("z", "core")
    n = lax.axis_size(slabs)
    up = [(i, i + 1) for i in range(n - 1)]
    down = [(i + 1, i) for i in range(n - 1)]
    tail = jnp.concatenate([field[:, 8:], rate[None, 8:], source[None, 8:]], axis=0)
    head = jnp.concatenate([field[:, :8], rate[None, :8], source[None, :8]], axis=0)
    bef = lax.ppermute(tail, slabs, up)
    aft = lax.ppermute(head, slabs, down)

    yt, *chunks = call(
        flow_kernel,
        (shape(64, 128),) + (shape(4, 64, 128),) * 4,
        1,
        step_counts,
        field.reshape(2048, 128),
        bef.reshape(1040, 128),
        aft.reshape(1040, 128),
        rate,
        source,
        amp,
        sketch_signs,
        scratch=[pltpu.VMEM((256, 128), F32)] * 4
        + [pltpu.VMEM((16, 128, 128), F32), pltpu.VMEM((4, 4, 64, 128), F32)],
    )
    got = [chunks[0]] + [shift(chunks[d], "y", d) for d in (1, 2, 3)]
    keep, send, sketches = call(
        cross_kernel,
        (shape(128, 128), shape(128, 128), shape(4, 4, 64, 128)),
        0,
        yt,
        *got,
        scratch=[pltpu.VMEM((192, 128), F32), pltpu.VMEM((2, 128, 128), F32)],
    )
    half = keep + shift(send, "core", 1)
    quarters = [half[32:56]] + [shift(half[32 + 24 * d : 56 + 24 * d], "y", d) for d in (1, 2, 3)]
    own = sum_over(jnp.concatenate([half[:32], total(quarters)], axis=0), "z")
    leaf = call(leaf_kernel, shape(112, 128), 0, own, shift(own, "core", 1), sketch_signs)
    piece = call(
        middle_kernel,
        shape(288, 128),
        0,
        *from_ring(leaf, "y"),
        sketches,
        sketch_signs,
        scratch=[pltpu.VMEM((4, 112, 128), F32), pltpu.VMEM((192, 128), F32)],
    )
    pieces = from_ring(piece, "x")
    s, keep, send = call(
        upper_kernel,
        (shape(2, 4, 64, 128), shape(48, 128), shape(48, 128)),
        0,
        *pieces,
        sketch_signs,
        scratch=[pltpu.VMEM((4, 256, 128), F32), pltpu.VMEM((2, 48, 128), F32)],
    )
    half = keep + shift(send, "core", 1)
    own = sum_over(total(from_ring(half, "y")), "z")
    out = call(
        last_kernel,
        shape(64, 128),
        0,
        own,
        shift(own, "core", 1),
        *pieces,
        s,
        sketch_signs,
        scratch=[pltpu.VMEM((4, 32, 128), F32)],
    )
    return out.reshape(64, 16, 8)


def solution(mesh):
    fine = Mesh(mesh.devices.reshape(4, 4, 8, 2), ("x", "y", "z", "core"))
    group, slab = ("x", "y"), ("z", "core")
    return jax.shard_map(
        per_device,
        mesh=fine,
        in_specs=(
            P(group, None, slab, None),
            P(group, slab, None),
            P(slab, None),
            P(),
            P(group, None),
            P(group),
            P(),
        ),
        out_specs=P(None, slab, group),
        check_vma=False,
    )
```

```python
import functools
import math

import jax
import jax.numpy as jnp
from jax import lax
from jax.experimental import pallas as pl
from jax.experimental.pallas import tpu as pltpu
from jax.sharding import Mesh
from jax.sharding import PartitionSpec as P

STEPS = 8
SCALE = 1.0 / math.sqrt(128.0)
HI = lax.Precision.HIGHEST
F32 = jnp.float32
VMEM = pl.BlockSpec(memory_space=pltpu.VMEM)
SMEM = pl.BlockSpec(memory_space=pltpu.SMEM)


def mm(a, b):
    return lax.dot_general(
        a, b, (((1,), (0,)), ((), ())), precision=HI, preferred_element_type=F32
    )


def mm_nt(a, b):
    return lax.dot_general(
        a, b, (((1,), (1,)), ((), ())), precision=HI, preferred_element_type=F32
    )


def thirds(x):
    hi = x.astype(jnp.bfloat16)
    rest = x - hi.astype(F32)
    mid = rest.astype(jnp.bfloat16)
    return hi, mid, (rest - mid.astype(F32)).astype(jnp.bfloat16)


def signs_mm(signs, x):
    hi, mid, lo = (jnp.dot(signs, t, preferred_element_type=F32) for t in thirds(x))
    return (hi + (mid + lo)) * SCALE


def mm_signs(x, signs):
    hi, mid, lo = (jnp.dot(t, signs, preferred_element_type=F32) for t in thirds(x))
    return (hi + (mid + lo)) * SCALE


def rows_of(v, i):
    return jnp.broadcast_to(v[i : i + 1, :], v.shape)


def factor(blocks, split):
    work = list(blocks)
    shape_of = work[0].shape
    sub = lax.broadcasted_iota(jnp.int32, shape_of, 0)
    lane = lax.broadcasted_iota(jnp.int32, shape_of, 1)
    base = jnp.where(lane < 64, 0, 64) if split else jnp.zeros(shape_of, jnp.int32)
    done = []
    for kb in range(8):
        cols = []
        for j in range(8):
            index = base + (8 * kb + j)
            cols.append([jnp.take_along_axis(work[i], index, axis=1) for i in range(kb, 8)])
        rows = [rows_of(work[kb], j) for j in range(8)]
        el = [[rows_of(cols[j][0], i) if i <= j else None for j in range(8)] for i in range(8)]
        outs, scaled = [], []
        for p in range(0, 8, 2):
            q = p + 1
            a, b, c = el[p][p], el[p][q], el[q][q]
            det = a * c - b * b
            inv = 1.0 / det
            rp, rq = rows[p], rows[q]
            root = lax.rsqrt(a)
            outs += [rp * root, (a * rq - b * rp) * (root * lax.rsqrt(det))]
            off = b * inv
            scaled += [(c * inv) * rp - off * rq, (a * inv) * rq - off * rp]
            left = {j: c * el[p][j] - b * el[q][j] for j in range(q + 1, 8)}
            right = {j: a * el[q][j] - b * el[p][j] for j in range(q + 1, 8)}
            for j in range(q + 1, 8):
                x, y = left[j] * inv, right[j] * inv
                for i in range(q + 1, j + 1):
                    el[i][j] = el[i][j] - (el[p][i] * left[j] + el[q][i] * right[j]) * inv
                rows[j] = rows[j] - (x * rp + y * rq)
                for n in range(1, 8 - kb):
                    cols[j][n] = cols[j][n] - (cols[p][n] * x + cols[q][n] * y)
        out = outs[0]
        for p in range(1, 8):
            out = jnp.where(sub == p, outs[p], out)
        done.append(out)
        for i in range(kb + 1, 8):
            acc = [cols[p][i - kb] * scaled[p] for p in range(8)]
            while len(acc) > 1:
                acc = [acc[2 * t] + acc[2 * t + 1] for t in range(len(acc) // 2)]
            work[i] = work[i] - acc[0]
    return jnp.concatenate(done, axis=0)


def shift_of(mat, diag):
    trace = jnp.sum(jnp.where(diag, mat, 0.0), keepdims=True)
    return jnp.where(diag, trace * (0.0001 / 64.0), 0.0)


def row_blocks(mat):
    return [mat[8 * i : 8 * i + 8] for i in range(8)]


def compress(yts, signs):
    row = lax.broadcasted_iota(jnp.int32, (64, 128), 0)
    lane = lax.broadcasted_iota(jnp.int32, (64, 128), 1)
    diag = lane == row
    wide = jnp.concatenate([signs, jnp.zeros((128, 64), jnp.bfloat16)], axis=1)
    moments = [mm_signs(yt, wide) for yt in yts]
    firsts = [
        factor(row_blocks(jnp.where(lane == row + 64, 1.0, m + shift_of(m, diag))), False)
        for m in moments
    ]
    linvs = [f[:, 64:] for f in firsts]
    hs = [mm(li, yt) for li, yt in zip(linvs, yts)]
    if len(hs) == 1:
        pad = jnp.zeros((64, 128), F32)
        inner = mm_nt(hs[0], jnp.concatenate([hs[0], pad], axis=0))
        inner = inner + shift_of(inner, diag)
        second = factor(row_blocks(inner), False)
        kts = [jnp.where(lane >= row, second, 0.0)[:, :64]]
    else:
        small = [mm_nt(h, h) for h in hs]
        small = [c + shift_of(c, diag[:, :64]) for c in small]
        second = factor(row_blocks(jnp.concatenate(small, axis=1)), True)
        second = jnp.where((lane & 63) >= row, second, 0.0)
        kts = [second[:, :64], second[:, 64:]]
    return [mm(k, li) for k, li in zip(kts, linvs)], [m[:, :64] for m in moments]


def gram_of(b, moment):
    return mm_nt(mm(b, moment), b)


def sketch_of_pair(first, cross, second, signs_t):
    top = jnp.concatenate([first, cross], axis=1)
    bottom = jnp.concatenate([cross.T, second], axis=1)
    return 0.5 * signs_mm(signs_t, jnp.concatenate([top, bottom], axis=0))


def signs_of(signs_refs, level):
    return signs_refs[0][level], signs_refs[1][level]


def both_halves(own_ref, other_ref):
    first = lax.axis_index("core") == 0
    own = own_ref[...]
    other = other_ref[...]
    return jnp.where(first, own, other), jnp.where(first, other, own)


def rest_of(value, by):
    return lax.rem(value + (by + 4), 4)


def exchange_blocks(vals, bit, lane_bit):
    lane = lax.broadcasted_iota(jnp.int32, vals[0].shape, 1)
    low = (lane & lane_bit) == 0
    out = list(vals)
    for i in range(len(vals)):
        if i & bit:
            continue
        a, b = vals[i], vals[i | bit]
        out[i] = jnp.where(low, a, pltpu.roll(b, lane_bit, 1))
        out[i | bit] = jnp.where(low, pltpu.roll(a, 128 - lane_bit, 1), b)
    return out


def advance(mid, above, below, rate, bend_rate, force, live):
    lane = lax.broadcasted_iota(jnp.int32, mid.shape, 1)
    left = jnp.where(lane != 0, pltpu.roll(mid, 1, 1), 0.0)
    right = jnp.where(lane != 127, pltpu.roll(mid, 127, 1), 0.0)
    lap = (below + above) + (right + left) - 4.0 * mid
    bend = jnp.tanh(mid)
    return jnp.where(live, mid + (rate + bend_rate * (bend * bend)) * lap + force, mid)


def spread_rows(at, rate, src, c_s, h_s, src_s):
    at = slice(8 * at, 8 * at + 8)
    c_s[at, :] = jnp.broadcast_to(rate, (8, 128))
    h_s[at, :] = jnp.broadcast_to(0.5 * rate, (8, 128))
    src_s[at, :] = jnp.broadcast_to(src, (8, 128))


def inner_kernel(
    count_ref, pick_ref, table_ref, x_ref, rate_ref, src_ref, bits_ref,
    last_ref, prev_ref, amp_ref, sg_ref, sgt_ref, c_s, h_s, src_s, f_s,
):
    for level in range(5):
        signs = 2.0 * bits_ref[level].astype(F32) - 1.0
        sg_ref[level] = signs.astype(jnp.bfloat16)
        sgt_ref[level] = signs.T.astype(jnp.bfloat16)
    for r in range(16):
        spread_rows(r, rate_ref[r : r + 1, :], src_ref[r : r + 1, :], c_s, h_s, src_s)
    count = count_ref[0]
    sub = lax.broadcasted_iota(jnp.int32, (8, 128), 0)

    def block(b, carry):
        rows = pl.ds(pl.multiple_of(b * 8, 8), 8)
        amp = jnp.zeros((8, 128), F32)
        for i in range(8):
            amp = jnp.where(sub == i, 0.1 * table_ref[pick_ref[0, 8 * b + i]], amp)
        amp_ref[rows, :] = amp
        old = [x_ref[pl.ds(b * 128 + r, 8, stride=16), :] for r in range(16)]
        for r in range(1, 15):
            f_s[8 * r : 8 * r + 8, :] = amp * src_s[8 * r : 8 * r + 8, :]
        for r in (0, 15):
            last_ref[r, rows, :] = old[r]
        for t in range(7):
            new = list(old)
            for r in range(t + 1, 15 - t):
                at = slice(8 * r, 8 * r + 8)
                new[r] = advance(
                    old[r], old[r - 1], old[r + 1], c_s[at, :], h_s[at, :], f_s[at, :], t < count
                )
            for r in (t + 1, 14 - t):
                prev_ref[r, rows, :] = old[r]
                last_ref[r, rows, :] = new[r]
            old = new
        return carry

    lax.fori_loop(0, 16, block, 0)


def flow_kernel(
    count_ref, last_ref, prev_ref, bef_ref, aft_ref, rate_ref, src_ref, amp_ref, sgt_ref,
    yt_ref, d0, d1, d2, d3, c_s, h_s, src_s, f_s, field_s, s_s,
):
    for r in range(32):
        if r < 8:
            rate, src = bef_ref[1024 + r : 1025 + r, :], bef_ref[1032 + r : 1033 + r, :]
        elif r < 24:
            rate, src = rate_ref[r - 8 : r - 7, :], src_ref[r - 8 : r - 7, :]
        else:
            rate, src = aft_ref[1000 + r : 1001 + r, :], aft_ref[1008 + r : 1009 + r, :]
        spread_rows(r, rate, src, c_s, h_s, src_s)
    count = count_ref[0]

    def block(b, carry):
        rows = pl.ds(pl.multiple_of(b * 8, 8), 8)
        amp = amp_ref[rows, :]
        for r in range(1, 31):
            f_s[8 * r : 8 * r + 8, :] = amp * src_s[8 * r : 8 * r + 8, :]
        low = {r - 8: bef_ref[pl.ds(b * 64 + r, 8, stride=8), :] for r in range(8)}
        high = {r + 16: aft_ref[pl.ds(b * 64 + r, 8, stride=8), :] for r in range(8)}
        for t in range(STEPS):
            low[t] = last_ref[t, rows, :]
            high[15 - t] = last_ref[15 - t, rows, :]
            low[t + 1] = last_ref[8, rows, :] if t == 7 else prev_ref[t + 1, rows, :]
            high[14 - t] = last_ref[7, rows, :] if t == 7 else prev_ref[14 - t, rows, :]
            sides = []
            for old, first in ((low, t - 7), (high, 15 - t)):
                new = {}
                for r in range(first, first + 8):
                    at = slice(8 * r + 64, 8 * r + 72)
                    new[r] = advance(
                        old[r], old[r - 1], old[r + 1], c_s[at, :], h_s[at, :], f_s[at, :], t < count
                    )
                sides.append(new)
            low, high = sides
        for r in range(8):
            field_s[r, rows, :] = low[r]
            field_s[8 + r, rows, :] = high[8 + r]
        return carry

    lax.fori_loop(0, 16, block, 0)
    signs_t = sgt_ref[0]
    yt = jnp.zeros((64, 128), F32)
    for q in range(4):
        parts = []
        for i in range(4):
            own = field_s[4 * q + i]
            sk = signs_mm(signs_t, own)
            yt = yt + mm_nt(sk, own)
            parts.append(sk)
        parts = exchange_blocks(exchange_blocks(parts, 1, 8), 2, 16)
        for j in range(4):
            s_s[j, q] = parts[j]
    yt_ref[...] = yt
    place = lax.axis_index("y")
    for d, out in enumerate((d0, d1, d2, d3)):
        out[...] = s_s[rest_of(place, d)]


def cross_kernel(yt_ref, r0, r1, r2, r3, keep_ref, send_ref, all_s, z_s, pay_s):
    place = lax.axis_index("y")
    for d, ref in enumerate((r0, r1, r2, r3)):
        all_s[rest_of(place, -d)] = ref[...]
    slabs = [jnp.zeros((64, 128), F32)] * 3
    for q in range(4):
        s0, s1, s2, s3 = (all_s[g, q] for g in range(4))
        upper = jnp.concatenate([s2, s3], axis=0)
        first = mm_nt(s0, jnp.concatenate([s1, s3], axis=0))
        slabs[1] = slabs[1] + mm_nt(s0, upper)
        slabs[2] = slabs[2] + mm_nt(s1, upper)
        slabs[0] = slabs[0] + jnp.concatenate([first[:, :64], mm_nt(s2, s3)], axis=1)
    for n in range(3):
        z_s[64 * n : 64 * n + 64] = slabs[n]
    for c in range(2):
        pay_s[c, 0:32] = yt_ref[32 * c : 32 * c + 32]
        for d in range(4):
            at = pl.multiple_of(48 * rest_of(place, d) + 24 * c, 8)
            pay_s[c, 32 + 24 * d : 56 + 24 * d] = z_s[pl.ds(at, 24), :]
    core = lax.axis_index("core")
    keep_ref[...] = pay_s[core]
    send_ref[...] = pay_s[1 - core]


def leaf_kernel(own_ref, other_ref, sg_ref, sgt_ref, out_ref):
    low, high = both_halves(own_ref, other_ref)
    signs, _ = signs_of((sg_ref, sgt_ref), 0)
    (b,), (moment,) = compress([jnp.concatenate([low[:32], high[:32]], axis=0)], signs)
    out_ref[0:64] = jnp.concatenate([b, gram_of(b, moment)], axis=1)
    out_ref[64:88] = low[32:]
    out_ref[88:112] = high[32:]


def middle_kernel(p0, p1, p2, p3, all_ref, sg_ref, sgt_ref, out_ref, pay_s, z_s):
    place = lax.axis_index("y")
    for d, ref in enumerate((p0, p1, p2, p3)):
        pay_s[rest_of(place, -d)] = ref[...]
    for g in range(4):
        z_s[48 * g : 48 * g + 48] = pay_s[g, 64:112]
    bs = [pay_s[g, 0:64][:, :64] for g in range(4)]
    grams = [pay_s[g, 0:64][:, 64:] for g in range(4)]
    inside = z_s[0:64]
    crosses = [mm_nt(mm(bs[0], inside[:, :64]), bs[1]), mm_nt(mm(bs[2], inside[:, 64:]), bs[3])]
    signs, signs_t = signs_of((sg_ref, sgt_ref), 1)
    yts = [
        sketch_of_pair(grams[2 * n], crosses[n], grams[2 * n + 1], signs_t) for n in range(2)
    ]
    ups, moments = compress(yts, signs)
    half = 0.5**0.5
    ws = []
    for n in range(2):
        low = signs_mm(signs_t[:, :64], bs[2 * n])
        high = signs_mm(signs_t[:, 64:], bs[2 * n + 1])
        ws.append(mm(ups[n], jnp.concatenate([low, high], axis=1)) * half)
    cross = mm_nt(mm(ws[0], z_s[64:192]), ws[1])
    signs, signs_t = signs_of((sg_ref, sgt_ref), 2)
    first, second = (gram_of(u, m) for u, m in zip(ups, moments))
    (b,), (moment,) = compress([sketch_of_pair(first, cross, second, signs_t)], signs)
    low = signs_mm(signs_t[:, :64], ws[0])
    high = signs_mm(signs_t[:, 64:], ws[1])
    w = mm(b, jnp.concatenate([low, high], axis=1)) * half
    for q in range(4):
        out_ref[64 * q : 64 * q + 64] = mm(
            w, jnp.concatenate([all_ref[g, q] for g in range(4)], axis=0)
        )
    gram = gram_of(b, moment)
    out_ref[256:288] = jnp.concatenate([gram[:32], gram[32:]], axis=1)


def upper_kernel(r0, r1, r2, r3, sg_ref, sgt_ref, s_ref, keep_ref, send_ref, all_s, pay_s):
    place = lax.axis_index("x")
    for d, ref in enumerate((r0, r1, r2, r3)):
        all_s[rest_of(place, -d)] = ref[0:256]
    _, signs_t = signs_of((sg_ref, sgt_ref), 3)
    slabs = [jnp.zeros((64, 64), F32)] * 3
    for q in range(4):
        at = slice(64 * q, 64 * q + 64)
        sks = []
        for n in range(2):
            low, high = all_s[2 * n, at], all_s[2 * n + 1, at]
            sk = signs_mm(signs_t, jnp.concatenate([low, high], axis=0)) * (0.5**0.5)
            s_ref[n, q] = sk
            sks.append(sk)
            slabs[n] = slabs[n] + mm_nt(low, high)
        slabs[2] = slabs[2] + mm_nt(*sks)
    for c in range(2):
        at = slice(32 * c, 32 * c + 32)
        pay_s[c, 0:32] = jnp.concatenate([slabs[0][at], slabs[1][at]], axis=1)
        pay_s[c, 32:48] = jnp.concatenate(
            [slabs[2][32 * c : 32 * c + 16], slabs[2][32 * c + 16 : 32 * c + 32]], axis=1
        )
    core = lax.axis_index("core")
    keep_ref[...] = pay_s[core]
    send_ref[...] = pay_s[1 - core]


def last_kernel(own_ref, other_ref, r0, r1, r2, r3, s_ref, sg_ref, sgt_ref, out_ref, gram_s):
    place = lax.axis_index("x")
    for d, ref in enumerate((r0, r1, r2, r3)):
        gram_s[rest_of(place, -d)] = ref[256:288]
    grams = []
    for g in range(4):
        packed = gram_s[g]
        grams.append(jnp.concatenate([packed[:, :64], packed[:, 64:]], axis=0))
    low, high = both_halves(own_ref, other_ref)
    pairs = jnp.concatenate([low[:32], high[:32]], axis=0)
    inside = jnp.concatenate(
        [low[32:, :64], low[32:, 64:], high[32:, :64], high[32:, 64:]], axis=0
    )
    signs, signs_t = signs_of((sg_ref, sgt_ref), 3)
    yts = [
        sketch_of_pair(grams[2 * n], pairs[:, 64 * n : 64 * n + 64], grams[2 * n + 1], signs_t)
        for n in range(2)
    ]
    bs, moments = compress(yts, signs)
    cross = mm_nt(mm(bs[0], inside), bs[1])
    first, second = (gram_of(u, m) for u, m in zip(bs, moments))
    signs, signs_t = signs_of((sg_ref, sgt_ref), 4)
    (b,), _ = compress([sketch_of_pair(first, cross, second, signs_t)], signs)
    lower = signs_mm(signs_t[:, :64], bs[0])
    upper = signs_mm(signs_t[:, 64:], bs[1])
    w = mm(b, jnp.concatenate([lower, upper], axis=1)) * (0.5**0.5)
    lane = lax.broadcasted_iota(jnp.int32, (128, 128), 1)
    block = lax.shift_right_logical(lane, 5)
    mine = jnp.zeros((128, 128), F32)
    for q in range(4):
        own = jnp.concatenate([s_ref[0, q], s_ref[1, q]], axis=0)
        turned = pltpu.roll(own, lax.rem(32 * q - 32 * place + 128, 128), 1)
        mine = jnp.where(block == q, turned, mine)
    out_ref[...] = mm(w, mine)


def call(kernel, out_shapes, smem, *args, scratch=(), limit=16, cost=None):
    specs = [SMEM] * smem + [VMEM] * (len(args) - smem)
    return pl.pallas_call(
        kernel,
        out_shape=out_shapes,
        in_specs=specs,
        out_specs=jax.tree.map(lambda _: VMEM, out_shapes),
        scratch_shapes=list(scratch),
        cost_estimate=cost,
        compiler_params=pltpu.CompilerParams(vmem_limit_bytes=limit << 20),
    )(*args)


def shape(*dims):
    return jax.ShapeDtypeStruct(dims, F32)


def shift(value, axis, by):
    n = lax.axis_size(axis)
    return lax.ppermute(value, axis, [(i, (i + by) % n) for i in range(n)])


def from_ring(value, axis):
    return [value] + [shift(value, axis, d) for d in (1, 2, 3)]


def total(parts):
    return (parts[0] + parts[1]) + (parts[2] + parts[3])


def sum_over(value, axis):
    peers = lax.axis_size(axis)
    sent = jnp.broadcast_to(value[None], (peers, *value.shape))
    return lax.all_to_all(sent, axis, 0, 0, tiled=True).sum(axis=0)


def per_device(init_state, coef, source, amplitudes, sample_idx, step_counts, sketch_signs):
    field = init_state[0]
    rate = coef[0]
    slabs = ("z", "core")
    n = lax.axis_size(slabs)
    up = [(i, i + 1) for i in range(n - 1)]
    down = [(i + 1, i) for i in range(n - 1)]
    tail = jnp.concatenate([field[:, 8:], rate[None, 8:], source[None, 8:]], axis=0)
    head = jnp.concatenate([field[:, :8], rate[None, :8], source[None, :8]], axis=0)
    bef = lax.ppermute(tail, slabs, up)
    aft = lax.ppermute(head, slabs, down)

    last, prev, amp, signs, signs_t = call(
        inner_kernel,
        (
            shape(16, 128, 128),
            shape(16, 128, 128),
            shape(128, 128),
            jax.ShapeDtypeStruct((5, 128, 64), jnp.bfloat16),
            jax.ShapeDtypeStruct((5, 64, 128), jnp.bfloat16),
        ),
        3,
        step_counts,
        sample_idx,
        amplitudes,
        field.reshape(2048, 128),
        rate,
        source,
        sketch_signs,
        scratch=[pltpu.VMEM((128, 128), F32)] * 4,
        cost=pl.CostEstimate(flops=4_000_000_000, bytes_accessed=4_000_000, transcendentals=0),
    )
    yt, *chunks = call(
        flow_kernel,
        (shape(64, 128),) + (shape(4, 64, 128),) * 4,
        1,
        step_counts,
        last,
        prev,
        bef.reshape(1040, 128),
        aft.reshape(1040, 128),
        rate,
        source,
        amp,
        signs_t,
        scratch=[pltpu.VMEM((256, 128), F32)] * 4
        + [pltpu.VMEM((16, 128, 128), F32), pltpu.VMEM((4, 4, 64, 128), F32)],
    )
    got = [chunks[0]] + [shift(chunks[d], "y", d) for d in (1, 2, 3)]
    keep, send, sketches = call(
        cross_kernel,
        (shape(128, 128), shape(128, 128), shape(4, 4, 64, 128)),
        0,
        yt,
        *got,
        scratch=[pltpu.VMEM((192, 128), F32), pltpu.VMEM((2, 128, 128), F32)],
    )
    half = keep + shift(send, "core", 1)
    quarters = [half[32:56]] + [shift(half[32 + 24 * d : 56 + 24 * d], "y", d) for d in (1, 2, 3)]
    own = sum_over(jnp.concatenate([half[:32], total(quarters)], axis=0), "z")
    leaf = call(leaf_kernel, shape(112, 128), 0, own, shift(own, "core", 1), signs, signs_t)
    piece = call(
        middle_kernel,
        shape(288, 128),
        0,
        *from_ring(leaf, "y"),
        sketches,
        signs,
        signs_t,
        scratch=[pltpu.VMEM((4, 112, 128), F32), pltpu.VMEM((192, 128), F32)],
    )
    pieces = from_ring(piece, "x")
    s, keep, send = call(
        upper_kernel,
        (shape(2, 4, 64, 128), shape(48, 128), shape(48, 128)),
        0,
        *pieces,
        signs,
        signs_t,
        scratch=[pltpu.VMEM((4, 256, 128), F32), pltpu.VMEM((2, 48, 128), F32)],
    )
    half = keep + shift(send, "core", 1)
    own = sum_over(total(from_ring(half, "y")), "z")
    out = call(
        last_kernel,
        shape(64, 128),
        0,
        own,
        shift(own, "core", 1),
        *pieces,
        s,
        signs,
        signs_t,
        scratch=[pltpu.VMEM((4, 32, 128), F32)],
    )
    return out.reshape(64, 16, 8)


def solution(mesh):
    fine = Mesh(mesh.devices.reshape(4, 4, 8, 2), ("x", "y", "z", "core"))
    group, slab = ("x", "y"), ("z", "core")
    return jax.shard_map(
        per_device,
        mesh=fine,
        in_specs=(
            P(group, None, slab, None),
            P(group, slab, None),
            P(slab, None),
            P(),
            P(group, None),
            P(group),
            P(),
        ),
        out_specs=P(None, slab, group),
        check_vma=False,
    )
```

```python
import functools
import math

import jax
import jax.numpy as jnp
from jax import lax
from jax.experimental import pallas as pl
from jax.experimental.pallas import tpu as pltpu
from jax.sharding import Mesh
from jax.sharding import PartitionSpec as P

STEPS = 8
SCALE = 1.0 / math.sqrt(128.0)
HI = lax.Precision.HIGHEST
F32 = jnp.float32
VMEM = pl.BlockSpec(memory_space=pltpu.VMEM)
SMEM = pl.BlockSpec(memory_space=pltpu.SMEM)


def mm(a, b):
    return lax.dot_general(
        a, b, (((1,), (0,)), ((), ())), precision=HI, preferred_element_type=F32
    )


def mm_nt(a, b):
    return lax.dot_general(
        a, b, (((1,), (1,)), ((), ())), precision=HI, preferred_element_type=F32
    )


def thirds(x):
    hi = x.astype(jnp.bfloat16)
    rest = x - hi.astype(F32)
    mid = rest.astype(jnp.bfloat16)
    return hi, mid, (rest - mid.astype(F32)).astype(jnp.bfloat16)


def signs_mm(signs, x):
    hi, mid, lo = (jnp.dot(signs, t, preferred_element_type=F32) for t in thirds(x))
    return (hi + (mid + lo)) * SCALE


def mm_signs(x, signs):
    hi, mid, lo = (jnp.dot(t, signs, preferred_element_type=F32) for t in thirds(x))
    return (hi + (mid + lo)) * SCALE


def rows_of(v, i):
    return jnp.broadcast_to(v[i : i + 1, :], v.shape)


def factor(blocks, split):
    work = list(blocks)
    shape_of = work[0].shape
    sub = lax.broadcasted_iota(jnp.int32, shape_of, 0)
    lane = lax.broadcasted_iota(jnp.int32, shape_of, 1)
    base = jnp.where(lane < 64, 0, 64) if split else jnp.zeros(shape_of, jnp.int32)
    done = []
    for kb in range(8):
        cols = []
        for j in range(8):
            index = base + (8 * kb + j)
            cols.append([jnp.take_along_axis(work[i], index, axis=1) for i in range(kb, 8)])
        rows = [rows_of(work[kb], j) for j in range(8)]
        el = [[rows_of(cols[j][0], i) if i <= j else None for j in range(8)] for i in range(8)]
        outs, scaled = [], []
        for p in range(0, 8, 2):
            q = p + 1
            a, b, c = el[p][p], el[p][q], el[q][q]
            det = a * c - b * b
            inv = 1.0 / det
            rp, rq = rows[p], rows[q]
            root = lax.rsqrt(a)
            outs += [rp * root, (a * rq - b * rp) * (root * lax.rsqrt(det))]
            off = b * inv
            scaled += [(c * inv) * rp - off * rq, (a * inv) * rq - off * rp]
            left = {j: c * el[p][j] - b * el[q][j] for j in range(q + 1, 8)}
            right = {j: a * el[q][j] - b * el[p][j] for j in range(q + 1, 8)}
            for j in range(q + 1, 8):
                x, y = left[j] * inv, right[j] * inv
                for i in range(q + 1, j + 1):
                    el[i][j] = el[i][j] - (el[p][i] * left[j] + el[q][i] * right[j]) * inv
                rows[j] = rows[j] - (x * rp + y * rq)
                for n in range(1, 8 - kb):
                    cols[j][n] = cols[j][n] - (cols[p][n] * x + cols[q][n] * y)
        out = outs[0]
        for p in range(1, 8):
            out = jnp.where(sub == p, outs[p], out)
        done.append(out)
        for i in range(kb + 1, 8):
            acc = [cols[p][i - kb] * scaled[p] for p in range(8)]
            while len(acc) > 1:
                acc = [acc[2 * t] + acc[2 * t + 1] for t in range(len(acc) // 2)]
            work[i] = work[i] - acc[0]
    return jnp.concatenate(done, axis=0)


def shift_of(mat, diag):
    trace = jnp.sum(jnp.where(diag, mat, 0.0), keepdims=True)
    return jnp.where(diag, trace * (0.0001 / 64.0), 0.0)


def row_blocks(mat):
    return [mat[8 * i : 8 * i + 8] for i in range(8)]


def compress(yts, signs):
    row = lax.broadcasted_iota(jnp.int32, (64, 128), 0)
    lane = lax.broadcasted_iota(jnp.int32, (64, 128), 1)
    diag = lane == row
    wide = jnp.concatenate([signs, jnp.zeros((128, 64), jnp.bfloat16)], axis=1)
    moments = [mm_signs(yt, wide) for yt in yts]
    firsts = [
        factor(row_blocks(jnp.where(lane == row + 64, 1.0, m + shift_of(m, diag))), False)
        for m in moments
    ]
    linvs = [f[:, 64:] for f in firsts]
    hs = [mm(li, yt) for li, yt in zip(linvs, yts)]
    if len(hs) == 1:
        pad = jnp.zeros((64, 128), F32)
        inner = mm_nt(hs[0], jnp.concatenate([hs[0], pad], axis=0))
        inner = inner + shift_of(inner, diag)
        second = factor(row_blocks(inner), False)
        kts = [jnp.where(lane >= row, second, 0.0)[:, :64]]
    else:
        small = [mm_nt(h, h) for h in hs]
        small = [c + shift_of(c, diag[:, :64]) for c in small]
        second = factor(row_blocks(jnp.concatenate(small, axis=1)), True)
        second = jnp.where((lane & 63) >= row, second, 0.0)
        kts = [second[:, :64], second[:, 64:]]
    return [mm(k, li) for k, li in zip(kts, linvs)], [m[:, :64] for m in moments]


def gram_of(b, moment):
    return mm_nt(mm(b, moment), b)


def sketch_of_pair(first, cross, second, signs_t):
    top = jnp.concatenate([first, cross], axis=1)
    bottom = jnp.concatenate([cross.T, second], axis=1)
    return 0.5 * signs_mm(signs_t, jnp.concatenate([top, bottom], axis=0))


def signs_of(signs_refs, level):
    return signs_refs[0][level], signs_refs[1][level]


def both_halves(own_ref, other_ref):
    first = lax.axis_index("core") == 0
    own = own_ref[...]
    other = other_ref[...]
    return jnp.where(first, own, other), jnp.where(first, other, own)


def rest_of(value, by):
    return lax.rem(value + (by + 4), 4)


def exchange_blocks(vals, bit, lane_bit):
    lane = lax.broadcasted_iota(jnp.int32, vals[0].shape, 1)
    low = (lane & lane_bit) == 0
    out = list(vals)
    for i in range(len(vals)):
        if i & bit:
            continue
        a, b = vals[i], vals[i | bit]
        out[i] = jnp.where(low, a, pltpu.roll(b, lane_bit, 1))
        out[i | bit] = jnp.where(low, pltpu.roll(a, 128 - lane_bit, 1), b)
    return out


def advance(mid, above, below, rate, bend_rate, force, live):
    lane = lax.broadcasted_iota(jnp.int32, mid.shape, 1)
    left = jnp.where(lane != 0, pltpu.roll(mid, 1, 1), 0.0)
    right = jnp.where(lane != 127, pltpu.roll(mid, 127, 1), 0.0)
    lap = (below + above) + (right + left) - 4.0 * mid
    bend = jnp.tanh(mid)
    return jnp.where(live, mid + (rate + bend_rate * (bend * bend)) * lap + force, mid)


def spread_rows(at, rate, src, c_s, h_s, src_s):
    at = slice(8 * at, 8 * at + 8)
    c_s[at, :] = jnp.broadcast_to(rate, (8, 128))
    h_s[at, :] = jnp.broadcast_to(0.5 * rate, (8, 128))
    src_s[at, :] = jnp.broadcast_to(src, (8, 128))


def turned(vals):
    sub = lax.broadcasted_iota(jnp.int32, vals[0].shape, 0)
    out = list(vals)
    for bit in (1, 2, 4):
        low = (sub & bit) == 0
        for i in range(8):
            if i & bit:
                continue
            a, b = out[i], out[i | bit]
            out[i] = jnp.where(low, a, pltpu.roll(b, bit, 0))
            out[i | bit] = jnp.where(low, pltpu.roll(a, 8 - bit, 0), b)
    return out


def pack_kernel(x_ref, rate_ref, src_ref, head_ref, tail_ref, x_s, sems):
    parts = [
        pltpu.make_async_copy(
            x_ref.at[pl.ds(512 * n, 512)], x_s.at[pl.ds(512 * n, 512)], sems.at[n]
        )
        for n in range(4)
    ]
    edges = []
    for half, out in enumerate((head_ref, tail_ref)):
        for n, ref in enumerate((rate_ref, src_ref)):
            edges.append(
                pltpu.make_async_copy(
                    ref.at[pl.ds(8 * half, 8)],
                    out.at[pl.ds(1024 + 8 * n, 8)],
                    sems.at[4 + len(edges)],
                )
            )
    for copy in parts + edges:
        copy.start()

    def block(b, carry):
        for half, out in enumerate((head_ref, tail_ref)):
            start = pl.multiple_of(b * 128, 8) + 8 * half
            vals = turned([x_s[pl.ds(start + 16 * i, 8), :] for i in range(8)])
            for r in range(8):
                out[pl.ds(pl.multiple_of(b * 8, 8) + 128 * r, 8), :] = vals[r]
        return carry

    for n in range(4):
        parts[n].wait()
        lax.fori_loop(4 * n, 4 * n + 4, block, 0)
    for copy in edges:
        copy.wait()


def inner_kernel(
    count_ref, pick_ref, table_ref, head_ref, tail_ref, bits_ref,
    last_ref, prev_ref, amp_ref, sg_ref, sgt_ref, c_s, h_s, src_s, f_s,
):
    for level in range(5):
        signs = 2.0 * bits_ref[level].astype(F32) - 1.0
        sg_ref[level] = signs.astype(jnp.bfloat16)
        sgt_ref[level] = signs.T.astype(jnp.bfloat16)
    for r in range(16):
        ref, at = (head_ref, 1024 + r) if r < 8 else (tail_ref, 1016 + r)
        spread_rows(r, ref[at : at + 1, :], ref[at + 8 : at + 9, :], c_s, h_s, src_s)
    count = count_ref[0]
    sub = lax.broadcasted_iota(jnp.int32, (8, 128), 0)

    def block(pair, carry):
        state = []
        for u in range(2):
            b = 2 * pair + u
            rows = pl.ds(pl.multiple_of(b * 8, 8), 8)
            amp = jnp.zeros((8, 128), F32)
            for i in range(8):
                amp = jnp.where(sub == i, 0.1 * table_ref[pick_ref[0, 8 * b + i]], amp)
            amp_ref[rows, :] = amp
            old = [
                ref[pl.ds(pl.multiple_of(b * 8, 8) + 128 * r, 8), :]
                for ref in (head_ref, tail_ref)
                for r in range(8)
            ]
            for r in range(1, 15):
                f_s[u, 8 * r : 8 * r + 8, :] = amp * src_s[8 * r : 8 * r + 8, :]
            for r in (0, 15):
                last_ref[r, rows, :] = old[r]
            state.append((rows, old))
        for t in range(7):
            stepped = []
            for u, (rows, old) in enumerate(state):
                new = list(old)
                for r in range(t + 1, 15 - t):
                    at = slice(8 * r, 8 * r + 8)
                    new[r] = advance(
                        old[r], old[r - 1], old[r + 1],
                        c_s[at, :], h_s[at, :], f_s[u, at, :], t < count,
                    )
                for r in (t + 1, 14 - t):
                    prev_ref[r, rows, :] = old[r]
                    last_ref[r, rows, :] = new[r]
                stepped.append((rows, new))
            state = stepped
        return carry

    lax.fori_loop(0, 8, block, 0)


def flow_kernel(
    count_ref, last_ref, prev_ref, bef_ref, aft_ref, head_ref, tail_ref, amp_ref, sgt_ref,
    field_ref, sk_ref, d0, d1, d2, d3, c_s, h_s, src_s, f_s, s_s,
):
    for r in range(32):
        ref = (bef_ref, head_ref, tail_ref, aft_ref)[r // 8]
        at = 1024 + r % 8
        rate, src = ref[at : at + 1, :], ref[at + 8 : at + 9, :]
        spread_rows(r, rate, src, c_s, h_s, src_s)
    count = count_ref[0]

    def block(pair, carry):
        state = []
        for u in range(2):
            start = pl.multiple_of(pair * 16 + 8 * u, 8)
            rows = pl.ds(start, 8)
            amp = amp_ref[rows, :]
            for r in range(1, 31):
                f_s[u, 8 * r : 8 * r + 8, :] = amp * src_s[8 * r : 8 * r + 8, :]
            low = {r - 8: bef_ref[pl.ds(start + 128 * r, 8), :] for r in range(8)}
            high = {r + 16: aft_ref[pl.ds(start + 128 * r, 8), :] for r in range(8)}
            state.append((rows, low, high))
        for t in range(STEPS):
            stepped = []
            for u, (rows, low, high) in enumerate(state):
                low[t] = last_ref[t, rows, :]
                high[15 - t] = last_ref[15 - t, rows, :]
                low[t + 1] = last_ref[8, rows, :] if t == 7 else prev_ref[t + 1, rows, :]
                high[14 - t] = last_ref[7, rows, :] if t == 7 else prev_ref[14 - t, rows, :]
                sides = []
                for old, first in ((low, t - 7), (high, 15 - t)):
                    new = {}
                    for r in range(first, first + 8):
                        at = slice(8 * r + 64, 8 * r + 72)
                        new[r] = advance(
                            old[r], old[r - 1], old[r + 1],
                            c_s[at, :], h_s[at, :], f_s[u, at, :], t < count,
                        )
                    sides.append(new)
                stepped.append((rows, *sides))
            state = stepped
        for rows, low, high in state:
            for r in range(8):
                field_ref[r, rows, :] = low[r]
                field_ref[8 + r, rows, :] = high[8 + r]
        return carry

    lax.fori_loop(0, 8, block, 0)
    signs_t = sgt_ref[0]
    for q in range(4):
        parts = []
        for i in range(4):
            sk = signs_mm(signs_t, field_ref[4 * q + i])
            sk_ref[4 * q + i] = sk
            parts.append(sk)
        parts = exchange_blocks(exchange_blocks(parts, 1, 8), 2, 16)
        for j in range(4):
            s_s[j, q] = parts[j]
    place = lax.axis_index("y")
    for d, out in enumerate((d0, d1, d2, d3)):
        out[...] = s_s[rest_of(place, d)]


def leaf_sum_kernel(field_ref, sk_ref, yt_ref):
    yt = jnp.zeros((64, 128), F32)
    for r in range(16):
        yt = yt + mm_nt(sk_ref[r], field_ref[r])
    yt_ref[...] = yt


def cross_kernel(yt_ref, r0, r1, r2, r3, keep_ref, send_ref, all_s, z_s, pay_s):
    place = lax.axis_index("y")
    for d, ref in enumerate((r0, r1, r2, r3)):
        all_s[rest_of(place, -d)] = ref[...]
    slabs = [jnp.zeros((64, 128), F32)] * 3
    for q in range(4):
        s0, s1, s2, s3 = (all_s[g, q] for g in range(4))
        upper = jnp.concatenate([s2, s3], axis=0)
        first = mm_nt(s0, jnp.concatenate([s1, s3], axis=0))
        slabs[1] = slabs[1] + mm_nt(s0, upper)
        slabs[2] = slabs[2] + mm_nt(s1, upper)
        slabs[0] = slabs[0] + jnp.concatenate([first[:, :64], mm_nt(s2, s3)], axis=1)
    for n in range(3):
        z_s[64 * n : 64 * n + 64] = slabs[n]
    for c in range(2):
        pay_s[c, 0:32] = yt_ref[32 * c : 32 * c + 32]
        for d in range(4):
            at = pl.multiple_of(48 * rest_of(place, d) + 24 * c, 8)
            pay_s[c, 32 + 24 * d : 56 + 24 * d] = z_s[pl.ds(at, 24), :]
    core = lax.axis_index("core")
    keep_ref[...] = pay_s[core]
    send_ref[...] = pay_s[1 - core]


def leaf_kernel(own_ref, other_ref, sg_ref, sgt_ref, out_ref):
    low, high = both_halves(own_ref, other_ref)
    signs, _ = signs_of((sg_ref, sgt_ref), 0)
    (b,), (moment,) = compress([jnp.concatenate([low[:32], high[:32]], axis=0)], signs)
    out_ref[0:64] = jnp.concatenate([b, gram_of(b, moment)], axis=1)
    out_ref[64:88] = low[32:]
    out_ref[88:112] = high[32:]


def middle_kernel(p0, p1, p2, p3, all_ref, sg_ref, sgt_ref, out_ref, pay_s, z_s):
    place = lax.axis_index("y")
    for d, ref in enumerate((p0, p1, p2, p3)):
        pay_s[rest_of(place, -d)] = ref[...]
    for g in range(4):
        z_s[48 * g : 48 * g + 48] = pay_s[g, 64:112]
    bs = [pay_s[g, 0:64][:, :64] for g in range(4)]
    grams = [pay_s[g, 0:64][:, 64:] for g in range(4)]
    inside = z_s[0:64]
    crosses = [mm_nt(mm(bs[0], inside[:, :64]), bs[1]), mm_nt(mm(bs[2], inside[:, 64:]), bs[3])]
    signs, signs_t = signs_of((sg_ref, sgt_ref), 1)
    yts = [
        sketch_of_pair(grams[2 * n], crosses[n], grams[2 * n + 1], signs_t) for n in range(2)
    ]
    ups, moments = compress(yts, signs)
    half = 0.5**0.5
    ws = []
    for n in range(2):
        low = signs_mm(signs_t[:, :64], bs[2 * n])
        high = signs_mm(signs_t[:, 64:], bs[2 * n + 1])
        ws.append(mm(ups[n], jnp.concatenate([low, high], axis=1)) * half)
    cross = mm_nt(mm(ws[0], z_s[64:192]), ws[1])
    signs, signs_t = signs_of((sg_ref, sgt_ref), 2)
    first, second = (gram_of(u, m) for u, m in zip(ups, moments))
    (b,), (moment,) = compress([sketch_of_pair(first, cross, second, signs_t)], signs)
    low = signs_mm(signs_t[:, :64], ws[0])
    high = signs_mm(signs_t[:, 64:], ws[1])
    w = mm(b, jnp.concatenate([low, high], axis=1)) * half
    for q in range(4):
        out_ref[64 * q : 64 * q + 64] = mm(
            w, jnp.concatenate([all_ref[g, q] for g in range(4)], axis=0)
        )
    gram = gram_of(b, moment)
    out_ref[256:288] = jnp.concatenate([gram[:32], gram[32:]], axis=1)


def upper_kernel(r0, r1, r2, r3, sg_ref, sgt_ref, s_ref, keep_ref, send_ref, all_s, pay_s):
    place = lax.axis_index("x")
    for d, ref in enumerate((r0, r1, r2, r3)):
        all_s[rest_of(place, -d)] = ref[0:256]
    _, signs_t = signs_of((sg_ref, sgt_ref), 3)
    slabs = [jnp.zeros((64, 64), F32)] * 3
    for q in range(4):
        at = slice(64 * q, 64 * q + 64)
        sks = []
        for n in range(2):
            low, high = all_s[2 * n, at], all_s[2 * n + 1, at]
            sk = signs_mm(signs_t, jnp.concatenate([low, high], axis=0)) * (0.5**0.5)
            s_ref[n, q] = sk
            sks.append(sk)
            slabs[n] = slabs[n] + mm_nt(low, high)
        slabs[2] = slabs[2] + mm_nt(*sks)
    for c in range(2):
        at = slice(32 * c, 32 * c + 32)
        pay_s[c, 0:32] = jnp.concatenate([slabs[0][at], slabs[1][at]], axis=1)
        pay_s[c, 32:48] = jnp.concatenate(
            [slabs[2][32 * c : 32 * c + 16], slabs[2][32 * c + 16 : 32 * c + 32]], axis=1
        )
    core = lax.axis_index("core")
    keep_ref[...] = pay_s[core]
    send_ref[...] = pay_s[1 - core]


def last_kernel(own_ref, other_ref, r0, r1, r2, r3, s_ref, sg_ref, sgt_ref, out_ref, gram_s):
    place = lax.axis_index("x")
    for d, ref in enumerate((r0, r1, r2, r3)):
        gram_s[rest_of(place, -d)] = ref[256:288]
    grams = []
    for g in range(4):
        packed = gram_s[g]
        grams.append(jnp.concatenate([packed[:, :64], packed[:, 64:]], axis=0))
    low, high = both_halves(own_ref, other_ref)
    pairs = jnp.concatenate([low[:32], high[:32]], axis=0)
    inside = jnp.concatenate(
        [low[32:, :64], low[32:, 64:], high[32:, :64], high[32:, 64:]], axis=0
    )
    signs, signs_t = signs_of((sg_ref, sgt_ref), 3)
    yts = [
        sketch_of_pair(grams[2 * n], pairs[:, 64 * n : 64 * n + 64], grams[2 * n + 1], signs_t)
        for n in range(2)
    ]
    bs, moments = compress(yts, signs)
    cross = mm_nt(mm(bs[0], inside), bs[1])
    first, second = (gram_of(u, m) for u, m in zip(bs, moments))
    signs, signs_t = signs_of((sg_ref, sgt_ref), 4)
    (b,), _ = compress([sketch_of_pair(first, cross, second, signs_t)], signs)
    lower = signs_mm(signs_t[:, :64], bs[0])
    upper = signs_mm(signs_t[:, 64:], bs[1])
    w = mm(b, jnp.concatenate([lower, upper], axis=1)) * (0.5**0.5)
    lane = lax.broadcasted_iota(jnp.int32, (128, 128), 1)
    block = lax.shift_right_logical(lane, 5)
    mine = jnp.zeros((128, 128), F32)
    for q in range(4):
        own = jnp.concatenate([s_ref[0, q], s_ref[1, q]], axis=0)
        turned = pltpu.roll(own, lax.rem(32 * q - 32 * place + 128, 128), 1)
        mine = jnp.where(block == q, turned, mine)
    out_ref[...] = mm(w, mine)


def call(kernel, out_shapes, smem, *args, scratch=(), limit=16, cost=None):
    specs = [SMEM] * smem + [VMEM] * (len(args) - smem)
    return pl.pallas_call(
        kernel,
        out_shape=out_shapes,
        in_specs=specs,
        out_specs=jax.tree.map(lambda _: VMEM, out_shapes),
        scratch_shapes=list(scratch),
        cost_estimate=cost,
        compiler_params=pltpu.CompilerParams(vmem_limit_bytes=limit << 20),
    )(*args)


def in_hbm(value):
    return pltpu.with_memory_space_constraint(value, pltpu.HBM)


def shape(*dims):
    return jax.ShapeDtypeStruct(dims, F32)


def shift(value, axis, by):
    n = lax.axis_size(axis)
    return lax.ppermute(value, axis, [(i, (i + by) % n) for i in range(n)])


def from_ring(value, axis):
    return [value] + [shift(value, axis, d) for d in (1, 2, 3)]


def total(parts):
    return (parts[0] + parts[1]) + (parts[2] + parts[3])


def sum_over(value, axis):
    peers = lax.axis_size(axis)
    sent = jnp.broadcast_to(value[None], (peers, *value.shape))
    return lax.all_to_all(sent, axis, 0, 0, tiled=True).sum(axis=0)


def per_device(init_state, coef, source, amplitudes, sample_idx, step_counts, sketch_signs):
    field = init_state[0]
    rate = coef[0]
    slabs = ("z", "core")
    n = lax.axis_size(slabs)
    up = [(i, i + 1) for i in range(n - 1)]
    down = [(i + 1, i) for i in range(n - 1)]
    head, tail = pl.pallas_call(
        pack_kernel,
        out_shape=(shape(1040, 128),) * 2,
        in_specs=[pl.BlockSpec(memory_space=pltpu.HBM)] * 3,
        out_specs=(VMEM, VMEM),
        scratch_shapes=[pltpu.VMEM((2048, 128), F32), pltpu.SemaphoreType.DMA((8,))],
        compiler_params=pltpu.CompilerParams(vmem_limit_bytes=16 << 20),
    )(*(in_hbm(v) for v in (field.reshape(2048, 128), rate, source)))
    bef = lax.ppermute(tail, slabs, up)
    aft = lax.ppermute(head, slabs, down)
    last, prev, amp, signs, signs_t = call(
        inner_kernel,
        (
            shape(16, 128, 128),
            shape(16, 128, 128),
            shape(128, 128),
            jax.ShapeDtypeStruct((5, 128, 64), jnp.bfloat16),
            jax.ShapeDtypeStruct((5, 64, 128), jnp.bfloat16),
        ),
        3,
        step_counts,
        sample_idx,
        amplitudes,
        head,
        tail,
        sketch_signs,
        scratch=[pltpu.VMEM((128, 128), F32)] * 3 + [pltpu.VMEM((2, 128, 128), F32)],
        cost=pl.CostEstimate(flops=4_000_000_000, bytes_accessed=4_000_000, transcendentals=0),
    )
    final, sks, *chunks = call(
        flow_kernel,
        (shape(16, 128, 128), shape(16, 64, 128)) + (shape(4, 64, 128),) * 4,
        1,
        step_counts,
        last,
        prev,
        bef,
        aft,
        head,
        tail,
        amp,
        signs_t,
        scratch=[pltpu.VMEM((256, 128), F32)] * 3
        + [pltpu.VMEM((2, 256, 128), F32), pltpu.VMEM((4, 4, 64, 128), F32)],
    )
    yt = call(
        leaf_sum_kernel,
        shape(64, 128),
        0,
        final,
        sks,
        cost=pl.CostEstimate(flops=2_000_000_000, bytes_accessed=2_000_000, transcendentals=0),
    )
    got = [chunks[0]] + [shift(chunks[d], "y", d) for d in (1, 2, 3)]
    keep, send, sketches = call(
        cross_kernel,
        (shape(128, 128), shape(128, 128), shape(4, 4, 64, 128)),
        0,
        yt,
        *got,
        scratch=[pltpu.VMEM((192, 128), F32), pltpu.VMEM((2, 128, 128), F32)],
    )
    half = keep + shift(send, "core", 1)
    quarters = [half[32:56]] + [shift(half[32 + 24 * d : 56 + 24 * d], "y", d) for d in (1, 2, 3)]
    own = sum_over(jnp.concatenate([half[:32], total(quarters)], axis=0), "z")
    leaf = call(leaf_kernel, shape(112, 128), 0, own, shift(own, "core", 1), signs, signs_t)
    piece = call(
        middle_kernel,
        shape(288, 128),
        0,
        *from_ring(leaf, "y"),
        sketches,
        signs,
        signs_t,
        scratch=[pltpu.VMEM((4, 112, 128), F32), pltpu.VMEM((192, 128), F32)],
    )
    pieces = from_ring(piece, "x")
    s, keep, send = call(
        upper_kernel,
        (shape(2, 4, 64, 128), shape(48, 128), shape(48, 128)),
        0,
        *pieces,
        signs,
        signs_t,
        scratch=[pltpu.VMEM((4, 256, 128), F32), pltpu.VMEM((2, 48, 128), F32)],
    )
    half = keep + shift(send, "core", 1)
    own = sum_over(total(from_ring(half, "y")), "z")
    out = call(
        last_kernel,
        shape(64, 128),
        0,
        own,
        shift(own, "core", 1),
        *pieces,
        s,
        signs,
        signs_t,
        scratch=[pltpu.VMEM((4, 32, 128), F32)],
    )
    return out.reshape(64, 16, 8)


def solution(mesh):
    fine = Mesh(mesh.devices.reshape(4, 4, 8, 2), ("x", "y", "z", "core"))
    group, slab = ("x", "y"), ("z", "core")
    return jax.shard_map(
        per_device,
        mesh=fine,
        in_specs=(
            P(group, None, slab, None),
            P(group, slab, None),
            P(slab, None),
            P(),
            P(group, None),
            P(group),
            P(),
        ),
        out_specs=P(None, slab, group),
        check_vma=False,
    )
```

```python
import functools
import math

import jax
import jax.numpy as jnp
from jax import lax
from jax.experimental import pallas as pl
from jax.experimental.pallas import tpu as pltpu
from jax.sharding import Mesh
from jax.sharding import PartitionSpec as P

STEPS = 8
SCALE = 1.0 / math.sqrt(128.0)
HI = lax.Precision.HIGHEST
F32 = jnp.float32
VMEM = pl.BlockSpec(memory_space=pltpu.VMEM)
SMEM = pl.BlockSpec(memory_space=pltpu.SMEM)


def mm(a, b):
    return lax.dot_general(
        a, b, (((1,), (0,)), ((), ())), precision=HI, preferred_element_type=F32
    )


def mm_nt(a, b):
    return lax.dot_general(
        a, b, (((1,), (1,)), ((), ())), precision=HI, preferred_element_type=F32
    )


def thirds(x):
    hi = x.astype(jnp.bfloat16)
    rest = x - hi.astype(F32)
    mid = rest.astype(jnp.bfloat16)
    return hi, mid, (rest - mid.astype(F32)).astype(jnp.bfloat16)


def signs_mm(signs, x):
    hi, mid, lo = (jnp.dot(signs, t, preferred_element_type=F32) for t in thirds(x))
    return (hi + (mid + lo)) * SCALE


def mm_signs(x, signs):
    hi, mid, lo = (jnp.dot(t, signs, preferred_element_type=F32) for t in thirds(x))
    return (hi + (mid + lo)) * SCALE


def rows_of(v, i):
    return jnp.broadcast_to(v[i : i + 1, :], v.shape)


def factor(blocks, split):
    work = list(blocks)
    shape_of = work[0].shape
    sub = lax.broadcasted_iota(jnp.int32, shape_of, 0)
    lane = lax.broadcasted_iota(jnp.int32, shape_of, 1)
    base = jnp.where(lane < 64, 0, 64) if split else jnp.zeros(shape_of, jnp.int32)
    done = []
    for kb in range(8):
        cols = []
        for j in range(8):
            index = base + (8 * kb + j)
            cols.append([jnp.take_along_axis(work[i], index, axis=1) for i in range(kb, 8)])
        rows = [rows_of(work[kb], j) for j in range(8)]
        el = [[rows_of(cols[j][0], i) if i <= j else None for j in range(8)] for i in range(8)]
        outs, scaled = [], []
        for p in range(0, 8, 2):
            q = p + 1
            a, b, c = el[p][p], el[p][q], el[q][q]
            det = a * c - b * b
            inv = 1.0 / det
            rp, rq = rows[p], rows[q]
            root = lax.rsqrt(a)
            outs += [rp * root, (a * rq - b * rp) * (root * lax.rsqrt(det))]
            off = b * inv
            scaled += [(c * inv) * rp - off * rq, (a * inv) * rq - off * rp]
            left = {j: c * el[p][j] - b * el[q][j] for j in range(q + 1, 8)}
            right = {j: a * el[q][j] - b * el[p][j] for j in range(q + 1, 8)}
            for j in range(q + 1, 8):
                x, y = left[j] * inv, right[j] * inv
                for i in range(q + 1, j + 1):
                    el[i][j] = el[i][j] - (el[p][i] * left[j] + el[q][i] * right[j]) * inv
                rows[j] = rows[j] - (x * rp + y * rq)
                for n in range(1, 8 - kb):
                    cols[j][n] = cols[j][n] - (cols[p][n] * x + cols[q][n] * y)
        out = outs[0]
        for p in range(1, 8):
            out = jnp.where(sub == p, outs[p], out)
        done.append(out)
        for i in range(kb + 1, 8):
            acc = [cols[p][i - kb] * scaled[p] for p in range(8)]
            while len(acc) > 1:
                acc = [acc[2 * t] + acc[2 * t + 1] for t in range(len(acc) // 2)]
            work[i] = work[i] - acc[0]
    return jnp.concatenate(done, axis=0)


def shift_of(mat, diag):
    trace = jnp.sum(jnp.where(diag, mat, 0.0), keepdims=True)
    return jnp.where(diag, trace * (0.0001 / 64.0), 0.0)


def row_blocks(mat):
    return [mat[8 * i : 8 * i + 8] for i in range(8)]


def compress(yts, signs):
    row = lax.broadcasted_iota(jnp.int32, (64, 128), 0)
    lane = lax.broadcasted_iota(jnp.int32, (64, 128), 1)
    diag = lane == row
    wide = jnp.concatenate([signs, jnp.zeros((128, 64), jnp.bfloat16)], axis=1)
    moments = [mm_signs(yt, wide) for yt in yts]
    firsts = [
        factor(row_blocks(jnp.where(lane == row + 64, 1.0, m + shift_of(m, diag))), False)
        for m in moments
    ]
    linvs = [f[:, 64:] for f in firsts]
    hs = [mm(li, yt) for li, yt in zip(linvs, yts)]
    if len(hs) == 1:
        pad = jnp.zeros((64, 128), F32)
        inner = mm_nt(hs[0], jnp.concatenate([hs[0], pad], axis=0))
        inner = inner + shift_of(inner, diag)
        second = factor(row_blocks(inner), False)
        kts = [jnp.where(lane >= row, second, 0.0)[:, :64]]
    else:
        small = [mm_nt(h, h) for h in hs]
        small = [c + shift_of(c, diag[:, :64]) for c in small]
        second = factor(row_blocks(jnp.concatenate(small, axis=1)), True)
        second = jnp.where((lane & 63) >= row, second, 0.0)
        kts = [second[:, :64], second[:, 64:]]
    return [mm(k, li) for k, li in zip(kts, linvs)], [m[:, :64] for m in moments]


def gram_of(b, moment):
    return mm_nt(mm(b, moment), b)


def sketch_of_pair(first, cross, second, signs_t):
    top = jnp.concatenate([first, cross], axis=1)
    bottom = jnp.concatenate([cross.T, second], axis=1)
    return 0.5 * signs_mm(signs_t, jnp.concatenate([top, bottom], axis=0))


def signs_of(signs_refs, level):
    return signs_refs[0][level], signs_refs[1][level]


def both_halves(own_ref, other_ref):
    first = lax.axis_index("core") == 0
    own = own_ref[...]
    other = other_ref[...]
    return jnp.where(first, own, other), jnp.where(first, other, own)


def rest_of(value, by):
    return lax.rem(value + (by + 4), 4)


def exchange_blocks(vals, bit, lane_bit):
    lane = lax.broadcasted_iota(jnp.int32, vals[0].shape, 1)
    low = (lane & lane_bit) == 0
    out = list(vals)
    for i in range(len(vals)):
        if i & bit:
            continue
        a, b = vals[i], vals[i | bit]
        out[i] = jnp.where(low, a, pltpu.roll(b, lane_bit, 1))
        out[i | bit] = jnp.where(low, pltpu.roll(a, 128 - lane_bit, 1), b)
    return out


def advance(mid, above, below, rate, bend_rate, force, live):
    lane = lax.broadcasted_iota(jnp.int32, mid.shape, 1)
    left = jnp.where(lane != 0, pltpu.roll(mid, 1, 1), 0.0)
    right = jnp.where(lane != 127, pltpu.roll(mid, 127, 1), 0.0)
    lap = (below + above) + (right + left) - 4.0 * mid
    bend = jnp.tanh(mid)
    return jnp.where(live, mid + (rate + bend_rate * (bend * bend)) * lap + force, mid)


def spread_rows(at, rate, src, c_s, h_s, src_s):
    at = slice(8 * at, 8 * at + 8)
    c_s[at, :] = jnp.broadcast_to(rate, (8, 128))
    h_s[at, :] = jnp.broadcast_to(0.5 * rate, (8, 128))
    src_s[at, :] = jnp.broadcast_to(src, (8, 128))


def turned(vals):
    sub = lax.broadcasted_iota(jnp.int32, vals[0].shape, 0)
    out = list(vals)
    for bit in (1, 2, 4):
        low = (sub & bit) == 0
        for i in range(8):
            if i & bit:
                continue
            a, b = out[i], out[i | bit]
            out[i] = jnp.where(low, a, pltpu.roll(b, bit, 0))
            out[i | bit] = jnp.where(low, pltpu.roll(a, 8 - bit, 0), b)
    return out


def pack_kernel(
    x_ref, rate_ref, src_ref, pick_ref, table_ref,
    head_ref, tail_ref, amp_ref, x_s, pick_s, table_s, sems,
):
    parts = [
        pltpu.make_async_copy(
            x_ref.at[pl.ds(512 * n, 512)], x_s.at[pl.ds(512 * n, 512)], sems.at[n]
        )
        for n in range(4)
    ]
    edges = []
    for half, out in enumerate((head_ref, tail_ref)):
        for n, ref in enumerate((rate_ref, src_ref)):
            edges.append(
                pltpu.make_async_copy(
                    ref.at[pl.ds(8 * half, 8)],
                    out.at[pl.ds(1024 + 8 * n, 8)],
                    sems.at[4 + len(edges)],
                )
            )
    tables = [
        pltpu.make_async_copy(pick_ref, pick_s, sems.at[8]),
        pltpu.make_async_copy(table_ref, table_s, sems.at[9]),
    ]
    for copy in parts + tables + edges:
        copy.start()
    for copy in tables:
        copy.wait()
    sub = lax.broadcasted_iota(jnp.int32, (8, 128), 0)

    def amplitude(b, carry):
        amp = jnp.zeros((8, 128), F32)
        for i in range(8):
            amp = jnp.where(sub == i, 0.1 * table_s[pick_s[0, 8 * b + i]], amp)
        amp_ref[pl.ds(pl.multiple_of(b * 8, 8), 8), :] = amp
        return carry

    lax.fori_loop(0, 16, amplitude, 0)

    def block(b, carry):
        for half, out in enumerate((head_ref, tail_ref)):
            start = pl.multiple_of(b * 128, 8) + 8 * half
            vals = turned([x_s[pl.ds(start + 16 * i, 8), :] for i in range(8)])
            for r in range(8):
                out[pl.ds(pl.multiple_of(b * 8, 8) + 128 * r, 8), :] = vals[r]
        return carry

    for n in range(4):
        parts[n].wait()
        lax.fori_loop(4 * n, 4 * n + 4, block, 0)
    for copy in edges:
        copy.wait()


def inner_kernel(
    count_ref, head_ref, tail_ref, amp_ref, bits_ref,
    last_ref, prev_ref, sgt_ref, c_s, h_s, src_s, f_s,
):
    sgt_ref[...] = (2.0 * bits_ref[0].astype(F32) - 1.0).astype(jnp.bfloat16)
    for r in range(16):
        ref, at = (head_ref, 1024 + r) if r < 8 else (tail_ref, 1016 + r)
        spread_rows(r, ref[at : at + 1, :], ref[at + 8 : at + 9, :], c_s, h_s, src_s)
    count = count_ref[0]

    def block(pair, carry):
        state = []
        for u in range(2):
            b = 2 * pair + u
            rows = pl.ds(pl.multiple_of(b * 8, 8), 8)
            amp = amp_ref[rows, :]
            old = [
                ref[pl.ds(pl.multiple_of(b * 8, 8) + 128 * r, 8), :]
                for ref in (head_ref, tail_ref)
                for r in range(8)
            ]
            for r in range(1, 15):
                f_s[u, 8 * r : 8 * r + 8, :] = amp * src_s[8 * r : 8 * r + 8, :]
            for r in (0, 15):
                last_ref[r, rows, :] = old[r]
            state.append((rows, old))
        for t in range(7):
            stepped = []
            for u, (rows, old) in enumerate(state):
                new = list(old)
                for r in range(t + 1, 15 - t):
                    at = slice(8 * r, 8 * r + 8)
                    new[r] = advance(
                        old[r], old[r - 1], old[r + 1],
                        c_s[at, :], h_s[at, :], f_s[u, at, :], t < count,
                    )
                for r in (t + 1, 14 - t):
                    prev_ref[r, rows, :] = old[r]
                    last_ref[r, rows, :] = new[r]
                stepped.append((rows, new))
            state = stepped
        return carry

    lax.fori_loop(0, 8, block, 0)


def flow_kernel(
    count_ref, last_ref, prev_ref, bef_ref, aft_ref, head_ref, tail_ref, amp_ref, sgt_ref,
    field_ref, sk_ref, d0, d1, d2, d3, c_s, h_s, src_s, f_s, s_s,
):
    for r in range(32):
        ref = (bef_ref, head_ref, tail_ref, aft_ref)[r // 8]
        at = 1024 + r % 8
        rate, src = ref[at : at + 1, :], ref[at + 8 : at + 9, :]
        spread_rows(r, rate, src, c_s, h_s, src_s)
    count = count_ref[0]

    def block(pair, carry):
        state = []
        for u in range(2):
            start = pl.multiple_of(pair * 16 + 8 * u, 8)
            rows = pl.ds(start, 8)
            amp = amp_ref[rows, :]
            for r in range(1, 31):
                f_s[u, 8 * r : 8 * r + 8, :] = amp * src_s[8 * r : 8 * r + 8, :]
            low = {r - 8: bef_ref[pl.ds(start + 128 * r, 8), :] for r in range(8)}
            high = {r + 16: aft_ref[pl.ds(start + 128 * r, 8), :] for r in range(8)}
            state.append((rows, low, high))
        for t in range(STEPS):
            stepped = []
            for u, (rows, low, high) in enumerate(state):
                low[t] = last_ref[t, rows, :]
                high[15 - t] = last_ref[15 - t, rows, :]
                low[t + 1] = last_ref[8, rows, :] if t == 7 else prev_ref[t + 1, rows, :]
                high[14 - t] = last_ref[7, rows, :] if t == 7 else prev_ref[14 - t, rows, :]
                sides = []
                for old, first in ((low, t - 7), (high, 15 - t)):
                    new = {}
                    for r in range(first, first + 8):
                        at = slice(8 * r + 64, 8 * r + 72)
                        new[r] = advance(
                            old[r], old[r - 1], old[r + 1],
                            c_s[at, :], h_s[at, :], f_s[u, at, :], t < count,
                        )
                    sides.append(new)
                stepped.append((rows, *sides))
            state = stepped
        for rows, low, high in state:
            for r in range(8):
                field_ref[r, rows, :] = low[r]
                field_ref[8 + r, rows, :] = high[8 + r]
        return carry

    lax.fori_loop(0, 8, block, 0)
    signs_t = sgt_ref[...]
    for q in range(4):
        parts = []
        for i in range(4):
            sk = signs_mm(signs_t, field_ref[4 * q + i])
            sk_ref[4 * q + i] = sk
            parts.append(sk)
        parts = exchange_blocks(exchange_blocks(parts, 1, 8), 2, 16)
        for j in range(4):
            s_s[j, q] = parts[j]
    place = lax.axis_index("y")
    for d, out in enumerate((d0, d1, d2, d3)):
        out[...] = s_s[rest_of(place, d)]


def leaf_sum_kernel(field_ref, sk_ref, bits_ref, yt_ref, sg_ref, sgt_ref):
    for level in range(5):
        signs = 2.0 * bits_ref[level].astype(F32) - 1.0
        sg_ref[level] = signs.T.astype(jnp.bfloat16)
        sgt_ref[level] = signs.astype(jnp.bfloat16)
    yt = jnp.zeros((64, 128), F32)
    for r in range(16):
        yt = yt + mm_nt(sk_ref[r], field_ref[r])
    yt_ref[...] = yt


def cross_kernel(yt_ref, r0, r1, r2, r3, keep_ref, send_ref, all_s, z_s, pay_s):
    place = lax.axis_index("y")
    for d, ref in enumerate((r0, r1, r2, r3)):
        all_s[rest_of(place, -d)] = ref[...]
    slabs = [jnp.zeros((64, 128), F32)] * 3
    for q in range(4):
        s0, s1, s2, s3 = (all_s[g, q] for g in range(4))
        upper = jnp.concatenate([s2, s3], axis=0)
        first = mm_nt(s0, jnp.concatenate([s1, s3], axis=0))
        slabs[1] = slabs[1] + mm_nt(s0, upper)
        slabs[2] = slabs[2] + mm_nt(s1, upper)
        slabs[0] = slabs[0] + jnp.concatenate([first[:, :64], mm_nt(s2, s3)], axis=1)
    for n in range(3):
        z_s[64 * n : 64 * n + 64] = slabs[n]
    for c in range(2):
        pay_s[c, 0:32] = yt_ref[32 * c : 32 * c + 32]
        for d in range(4):
            at = pl.multiple_of(48 * rest_of(place, d) + 24 * c, 8)
            pay_s[c, 32 + 24 * d : 56 + 24 * d] = z_s[pl.ds(at, 24), :]
    core = lax.axis_index("core")
    keep_ref[...] = pay_s[core]
    send_ref[...] = pay_s[1 - core]


def leaf_kernel(own_ref, other_ref, sg_ref, sgt_ref, out_ref):
    low, high = both_halves(own_ref, other_ref)
    signs, _ = signs_of((sg_ref, sgt_ref), 0)
    (b,), (moment,) = compress([jnp.concatenate([low[:32], high[:32]], axis=0)], signs)
    out_ref[0:64] = jnp.concatenate([b, gram_of(b, moment)], axis=1)
    out_ref[64:88] = low[32:]
    out_ref[88:112] = high[32:]


def middle_kernel(p0, p1, p2, p3, all_ref, sg_ref, sgt_ref, out_ref, pay_s, z_s):
    place = lax.axis_index("y")
    for d, ref in enumerate((p0, p1, p2, p3)):
        pay_s[rest_of(place, -d)] = ref[...]
    for g in range(4):
        z_s[48 * g : 48 * g + 48] = pay_s[g, 64:112]
    bs = [pay_s[g, 0:64][:, :64] for g in range(4)]
    grams = [pay_s[g, 0:64][:, 64:] for g in range(4)]
    inside = z_s[0:64]
    crosses = [mm_nt(mm(bs[0], inside[:, :64]), bs[1]), mm_nt(mm(bs[2], inside[:, 64:]), bs[3])]
    signs, signs_t = signs_of((sg_ref, sgt_ref), 1)
    yts = [
        sketch_of_pair(grams[2 * n], crosses[n], grams[2 * n + 1], signs_t) for n in range(2)
    ]
    ups, moments = compress(yts, signs)
    half = 0.5**0.5
    ws = []
    for n in range(2):
        low = signs_mm(signs_t[:, :64], bs[2 * n])
        high = signs_mm(signs_t[:, 64:], bs[2 * n + 1])
        ws.append(mm(ups[n], jnp.concatenate([low, high], axis=1)) * half)
    cross = mm_nt(mm(ws[0], z_s[64:192]), ws[1])
    signs, signs_t = signs_of((sg_ref, sgt_ref), 2)
    first, second = (gram_of(u, m) for u, m in zip(ups, moments))
    (b,), (moment,) = compress([sketch_of_pair(first, cross, second, signs_t)], signs)
    low = signs_mm(signs_t[:, :64], ws[0])
    high = signs_mm(signs_t[:, 64:], ws[1])
    w = mm(b, jnp.concatenate([low, high], axis=1)) * half
    for q in range(4):
        out_ref[64 * q : 64 * q + 64] = mm(
            w, jnp.concatenate([all_ref[g, q] for g in range(4)], axis=0)
        )
    gram = gram_of(b, moment)
    out_ref[256:288] = jnp.concatenate([gram[:32], gram[32:]], axis=1)


def upper_kernel(r0, r1, r2, r3, sg_ref, sgt_ref, s_ref, keep_ref, send_ref, all_s, pay_s):
    place = lax.axis_index("x")
    for d, ref in enumerate((r0, r1, r2, r3)):
        all_s[rest_of(place, -d)] = ref[0:256]
    _, signs_t = signs_of((sg_ref, sgt_ref), 3)
    slabs = [jnp.zeros((64, 64), F32)] * 3
    for q in range(4):
        at = slice(64 * q, 64 * q + 64)
        sks = []
        for n in range(2):
            low, high = all_s[2 * n, at], all_s[2 * n + 1, at]
            sk = signs_mm(signs_t, jnp.concatenate([low, high], axis=0)) * (0.5**0.5)
            s_ref[n, q] = sk
            sks.append(sk)
            slabs[n] = slabs[n] + mm_nt(low, high)
        slabs[2] = slabs[2] + mm_nt(*sks)
    for c in range(2):
        at = slice(32 * c, 32 * c + 32)
        pay_s[c, 0:32] = jnp.concatenate([slabs[0][at], slabs[1][at]], axis=1)
        pay_s[c, 32:48] = jnp.concatenate(
            [slabs[2][32 * c : 32 * c + 16], slabs[2][32 * c + 16 : 32 * c + 32]], axis=1
        )
    core = lax.axis_index("core")
    keep_ref[...] = pay_s[core]
    send_ref[...] = pay_s[1 - core]


def last_kernel(own_ref, other_ref, r0, r1, r2, r3, s_ref, sg_ref, sgt_ref, out_ref, gram_s):
    place = lax.axis_index("x")
    for d, ref in enumerate((r0, r1, r2, r3)):
        gram_s[rest_of(place, -d)] = ref[256:288]
    grams = []
    for g in range(4):
        packed = gram_s[g]
        grams.append(jnp.concatenate([packed[:, :64], packed[:, 64:]], axis=0))
    low, high = both_halves(own_ref, other_ref)
    pairs = jnp.concatenate([low[:32], high[:32]], axis=0)
    inside = jnp.concatenate(
        [low[32:, :64], low[32:, 64:], high[32:, :64], high[32:, 64:]], axis=0
    )
    signs, signs_t = signs_of((sg_ref, sgt_ref), 3)
    yts = [
        sketch_of_pair(grams[2 * n], pairs[:, 64 * n : 64 * n + 64], grams[2 * n + 1], signs_t)
        for n in range(2)
    ]
    bs, moments = compress(yts, signs)
    cross = mm_nt(mm(bs[0], inside), bs[1])
    first, second = (gram_of(u, m) for u, m in zip(bs, moments))
    signs, signs_t = signs_of((sg_ref, sgt_ref), 4)
    (b,), _ = compress([sketch_of_pair(first, cross, second, signs_t)], signs)
    lower = signs_mm(signs_t[:, :64], bs[0])
    upper = signs_mm(signs_t[:, 64:], bs[1])
    w = mm(b, jnp.concatenate([lower, upper], axis=1)) * (0.5**0.5)
    lane = lax.broadcasted_iota(jnp.int32, (128, 128), 1)
    block = lax.shift_right_logical(lane, 5)
    mine = jnp.zeros((128, 128), F32)
    for q in range(4):
        own = jnp.concatenate([s_ref[0, q], s_ref[1, q]], axis=0)
        turned = pltpu.roll(own, lax.rem(32 * q - 32 * place + 128, 128), 1)
        mine = jnp.where(block == q, turned, mine)
    out_ref[...] = mm(w, mine)


def call(kernel, out_shapes, smem, *args, scratch=(), limit=16, cost=None):
    specs = [SMEM] * smem + [VMEM] * (len(args) - smem)
    return pl.pallas_call(
        kernel,
        out_shape=out_shapes,
        in_specs=specs,
        out_specs=jax.tree.map(lambda _: VMEM, out_shapes),
        scratch_shapes=list(scratch),
        cost_estimate=cost,
        compiler_params=pltpu.CompilerParams(vmem_limit_bytes=limit << 20),
    )(*args)


def in_hbm(value):
    return pltpu.with_memory_space_constraint(value, pltpu.HBM)


def shape(*dims):
    return jax.ShapeDtypeStruct(dims, F32)


def shift(value, axis, by):
    n = lax.axis_size(axis)
    return lax.ppermute(value, axis, [(i, (i + by) % n) for i in range(n)])


def from_ring(value, axis):
    return [value] + [shift(value, axis, d) for d in (1, 2, 3)]


def total(parts):
    return (parts[0] + parts[1]) + (parts[2] + parts[3])


def sum_over(value, axis):
    peers = lax.axis_size(axis)
    sent = jnp.broadcast_to(value[None], (peers, *value.shape))
    return lax.all_to_all(sent, axis, 0, 0, tiled=True).sum(axis=0)


def per_device(init_state, coef, source, amplitudes, sample_idx, step_counts, sketch_signs):
    field = init_state[0]
    rate = coef[0]
    slabs = ("z", "core")
    n = lax.axis_size(slabs)
    up = [(i, i + 1) for i in range(n - 1)]
    down = [(i + 1, i) for i in range(n - 1)]
    head, tail, amp = pl.pallas_call(
        pack_kernel,
        out_shape=(shape(1040, 128), shape(1040, 128), shape(128, 128)),
        in_specs=[pl.BlockSpec(memory_space=pltpu.HBM)] * 5,
        out_specs=(VMEM,) * 3,
        scratch_shapes=[
            pltpu.VMEM((2048, 128), F32),
            pltpu.SMEM((1, 128), jnp.int32),
            pltpu.SMEM((64,), F32),
            pltpu.SemaphoreType.DMA((10,)),
        ],
        compiler_params=pltpu.CompilerParams(vmem_limit_bytes=16 << 20),
    )(
        *(
            in_hbm(v)
            for v in (field.reshape(2048, 128), rate, source, sample_idx, amplitudes)
        )
    )
    bits = jnp.swapaxes(sketch_signs, 1, 2)
    bef = lax.ppermute(tail, slabs, up)
    aft = lax.ppermute(head, slabs, down)
    last, prev, first_signs = call(
        inner_kernel,
        (
            shape(16, 128, 128),
            shape(16, 128, 128),
            jax.ShapeDtypeStruct((64, 128), jnp.bfloat16),
        ),
        1,
        step_counts,
        head,
        tail,
        amp,
        bits,
        scratch=[pltpu.VMEM((128, 128), F32)] * 3 + [pltpu.VMEM((2, 128, 128), F32)],
        cost=pl.CostEstimate(flops=4_000_000_000, bytes_accessed=4_000_000, transcendentals=0),
    )
    final, sks, *chunks = call(
        flow_kernel,
        (shape(16, 128, 128), shape(16, 64, 128)) + (shape(4, 64, 128),) * 4,
        1,
        step_counts,
        last,
        prev,
        bef,
        aft,
        head,
        tail,
        amp,
        first_signs,
        scratch=[pltpu.VMEM((256, 128), F32)] * 3
        + [pltpu.VMEM((2, 256, 128), F32), pltpu.VMEM((4, 4, 64, 128), F32)],
    )
    yt, signs, signs_t = call(
        leaf_sum_kernel,
        (
            shape(64, 128),
            jax.ShapeDtypeStruct((5, 128, 64), jnp.bfloat16),
            jax.ShapeDtypeStruct((5, 64, 128), jnp.bfloat16),
        ),
        0,
        final,
        sks,
        bits,
        cost=pl.CostEstimate(flops=2_000_000_000, bytes_accessed=2_000_000, transcendentals=0),
    )
    got = [chunks[0]] + [shift(chunks[d], "y", d) for d in (1, 2, 3)]
    keep, send, sketches = call(
        cross_kernel,
        (shape(128, 128), shape(128, 128), shape(4, 4, 64, 128)),
        0,
        yt,
        *got,
        scratch=[pltpu.VMEM((192, 128), F32), pltpu.VMEM((2, 128, 128), F32)],
    )
    half = keep + shift(send, "core", 1)
    quarters = [half[32:56]] + [shift(half[32 + 24 * d : 56 + 24 * d], "y", d) for d in (1, 2, 3)]
    own = sum_over(jnp.concatenate([half[:32], total(quarters)], axis=0), "z")
    leaf = call(leaf_kernel, shape(112, 128), 0, own, shift(own, "core", 1), signs, signs_t)
    piece = call(
        middle_kernel,
        shape(288, 128),
        0,
        *from_ring(leaf, "y"),
        sketches,
        signs,
        signs_t,
        scratch=[pltpu.VMEM((4, 112, 128), F32), pltpu.VMEM((192, 128), F32)],
    )
    pieces = from_ring(piece, "x")
    s, keep, send = call(
        upper_kernel,
        (shape(2, 4, 64, 128), shape(48, 128), shape(48, 128)),
        0,
        *pieces,
        signs,
        signs_t,
        scratch=[pltpu.VMEM((4, 256, 128), F32), pltpu.VMEM((2, 48, 128), F32)],
    )
    half = keep + shift(send, "core", 1)
    own = sum_over(total(from_ring(half, "y")), "z")
    out = call(
        last_kernel,
        shape(64, 128),
        0,
        own,
        shift(own, "core", 1),
        *pieces,
        s,
        signs,
        signs_t,
        scratch=[pltpu.VMEM((4, 32, 128), F32)],
    )
    return out.reshape(64, 16, 8)


def solution(mesh):
    fine = Mesh(mesh.devices.reshape(4, 4, 8, 2), ("x", "y", "z", "core"))
    group, slab = ("x", "y"), ("z", "core")
    return jax.shard_map(
        per_device,
        mesh=fine,
        in_specs=(
            P(group, None, slab, None),
            P(group, slab, None),
            P(slab, None),
            P(),
            P(group, None),
            P(group),
            P(),
        ),
        out_specs=P(None, slab, group),
        check_vma=False,
    )
```

```python
import functools
import math

import jax
import jax.numpy as jnp
from jax import lax
from jax.experimental import pallas as pl
from jax.experimental.pallas import tpu as pltpu
from jax.sharding import Mesh
from jax.sharding import PartitionSpec as P

STEPS = 8
SCALE = 1.0 / math.sqrt(128.0)
HI = lax.Precision.HIGHEST
F32 = jnp.float32
VMEM = pl.BlockSpec(memory_space=pltpu.VMEM)
SMEM = pl.BlockSpec(memory_space=pltpu.SMEM)


def mm(a, b):
    return lax.dot_general(
        a, b, (((1,), (0,)), ((), ())), precision=HI, preferred_element_type=F32
    )


def mm_nt(a, b):
    return lax.dot_general(
        a, b, (((1,), (1,)), ((), ())), precision=HI, preferred_element_type=F32
    )


def thirds(x):
    hi = x.astype(jnp.bfloat16)
    rest = x - hi.astype(F32)
    mid = rest.astype(jnp.bfloat16)
    return hi, mid, (rest - mid.astype(F32)).astype(jnp.bfloat16)


def signs_mm(signs, x):
    hi, mid, lo = (jnp.dot(signs, t, preferred_element_type=F32) for t in thirds(x))
    return (hi + (mid + lo)) * SCALE


def mm_signs(x, signs):
    hi, mid, lo = (jnp.dot(t, signs, preferred_element_type=F32) for t in thirds(x))
    return (hi + (mid + lo)) * SCALE


def rows_of(v, i):
    return jnp.broadcast_to(v[i : i + 1, :], v.shape)


def factor(blocks, split):
    work = list(blocks)
    shape_of = work[0].shape
    sub = lax.broadcasted_iota(jnp.int32, shape_of, 0)
    lane = lax.broadcasted_iota(jnp.int32, shape_of, 1)
    base = jnp.where(lane < 64, 0, 64) if split else jnp.zeros(shape_of, jnp.int32)
    done = []
    for kb in range(8):
        cols = []
        for j in range(8):
            index = base + (8 * kb + j)
            cols.append([jnp.take_along_axis(work[i], index, axis=1) for i in range(kb, 8)])
        rows = [rows_of(work[kb], j) for j in range(8)]
        el = [[rows_of(cols[j][0], i) if i <= j else None for j in range(8)] for i in range(8)]
        outs, scaled = [], []
        for p in range(0, 8, 2):
            q = p + 1
            a, b, c = el[p][p], el[p][q], el[q][q]
            det = a * c - b * b
            inv = 1.0 / det
            rp, rq = rows[p], rows[q]
            root = lax.rsqrt(a)
            outs += [rp * root, (a * rq - b * rp) * (root * lax.rsqrt(det))]
            off = b * inv
            scaled += [(c * inv) * rp - off * rq, (a * inv) * rq - off * rp]
            left = {j: c * el[p][j] - b * el[q][j] for j in range(q + 1, 8)}
            right = {j: a * el[q][j] - b * el[p][j] for j in range(q + 1, 8)}
            for j in range(q + 1, 8):
                x, y = left[j] * inv, right[j] * inv
                for i in range(q + 1, j + 1):
                    el[i][j] = el[i][j] - (el[p][i] * left[j] + el[q][i] * right[j]) * inv
                rows[j] = rows[j] - (x * rp + y * rq)
                for n in range(1, 8 - kb):
                    cols[j][n] = cols[j][n] - (cols[p][n] * x + cols[q][n] * y)
        out = outs[0]
        for p in range(1, 8):
            out = jnp.where(sub == p, outs[p], out)
        done.append(out)
        for i in range(kb + 1, 8):
            acc = [cols[p][i - kb] * scaled[p] for p in range(8)]
            while len(acc) > 1:
                acc = [acc[2 * t] + acc[2 * t + 1] for t in range(len(acc) // 2)]
            work[i] = work[i] - acc[0]
    return jnp.concatenate(done, axis=0)


def shift_of(mat, diag):
    trace = jnp.sum(jnp.where(diag, mat, 0.0), keepdims=True)
    return jnp.where(diag, trace * (0.0001 / 64.0), 0.0)


def row_blocks(mat):
    return [mat[8 * i : 8 * i + 8] for i in range(8)]


def compress(yts, signs):
    row = lax.broadcasted_iota(jnp.int32, (64, 128), 0)
    lane = lax.broadcasted_iota(jnp.int32, (64, 128), 1)
    diag = lane == row
    wide = jnp.concatenate([signs, jnp.zeros((128, 64), jnp.bfloat16)], axis=1)
    moments = [mm_signs(yt, wide) for yt in yts]
    firsts = [
        factor(row_blocks(jnp.where(lane == row + 64, 1.0, m + shift_of(m, diag))), False)
        for m in moments
    ]
    linvs = [f[:, 64:] for f in firsts]
    hs = [mm(li, yt) for li, yt in zip(linvs, yts)]
    if len(hs) == 1:
        pad = jnp.zeros((64, 128), F32)
        inner = mm_nt(hs[0], jnp.concatenate([hs[0], pad], axis=0))
        inner = inner + shift_of(inner, diag)
        second = factor(row_blocks(inner), False)
        kts = [jnp.where(lane >= row, second, 0.0)[:, :64]]
    else:
        small = [mm_nt(h, h) for h in hs]
        small = [c + shift_of(c, diag[:, :64]) for c in small]
        second = factor(row_blocks(jnp.concatenate(small, axis=1)), True)
        second = jnp.where((lane & 63) >= row, second, 0.0)
        kts = [second[:, :64], second[:, 64:]]
    return [mm(k, li) for k, li in zip(kts, linvs)], [m[:, :64] for m in moments]


def gram_of(b, moment):
    return mm_nt(mm(b, moment), b)


def sketch_of_pair(first, cross, second, signs_t):
    top = jnp.concatenate([first, cross], axis=1)
    bottom = jnp.concatenate([cross.T, second], axis=1)
    return 0.5 * signs_mm(signs_t, jnp.concatenate([top, bottom], axis=0))


def signs_of(signs_refs, level):
    return signs_refs[0][level], signs_refs[1][level]


def both_halves(own_ref, other_ref):
    first = lax.axis_index("core") == 0
    own = own_ref[...]
    other = other_ref[...]
    return jnp.where(first, own, other), jnp.where(first, other, own)


def rest_of(value, by):
    return lax.rem(value + (by + 4), 4)


def exchange_blocks(vals, bit, lane_bit):
    lane = lax.broadcasted_iota(jnp.int32, vals[0].shape, 1)
    low = (lane & lane_bit) == 0
    out = list(vals)
    for i in range(len(vals)):
        if i & bit:
            continue
        a, b = vals[i], vals[i | bit]
        out[i] = jnp.where(low, a, pltpu.roll(b, lane_bit, 1))
        out[i | bit] = jnp.where(low, pltpu.roll(a, 128 - lane_bit, 1), b)
    return out


def advance(mid, above, below, rate, bend_rate, force, live):
    lane = lax.broadcasted_iota(jnp.int32, mid.shape, 1)
    left = jnp.where(lane != 0, pltpu.roll(mid, 1, 1), 0.0)
    right = jnp.where(lane != 127, pltpu.roll(mid, 127, 1), 0.0)
    lap = (below + above) + (right + left) - 4.0 * mid
    bend = jnp.tanh(mid)
    return jnp.where(live, mid + (rate + bend_rate * (bend * bend)) * lap + force, mid)


def spread_rows(at, rate, src, c_s, h_s, src_s):
    at = slice(8 * at, 8 * at + 8)
    c_s[at, :] = jnp.broadcast_to(rate, (8, 128))
    h_s[at, :] = jnp.broadcast_to(0.5 * rate, (8, 128))
    src_s[at, :] = jnp.broadcast_to(src, (8, 128))


def turned(vals):
    sub = lax.broadcasted_iota(jnp.int32, vals[0].shape, 0)
    out = list(vals)
    for bit in (1, 2, 4):
        low = (sub & bit) == 0
        for i in range(8):
            if i & bit:
                continue
            a, b = out[i], out[i | bit]
            out[i] = jnp.where(low, a, pltpu.roll(b, bit, 0))
            out[i | bit] = jnp.where(low, pltpu.roll(a, 8 - bit, 0), b)
    return out


def pack_kernel(
    x_ref, rate_ref, src_ref, pick_ref, table_ref,
    ends_ref, cross_ref, chip_ref, amp_ref, x_s, pick_s, table_s, sems,
):
    parts = [
        pltpu.make_async_copy(
            x_ref.at[pl.ds(512 * n, 512)], x_s.at[pl.ds(512 * n, 512)], sems.at[n]
        )
        for n in range(4)
    ]
    edges = []
    for half, out in enumerate((ends_ref.at[0], ends_ref.at[1])):
        for n, ref in enumerate((rate_ref, src_ref)):
            edges.append(
                pltpu.make_async_copy(
                    ref.at[pl.ds(8 * half, 8)],
                    out.at[pl.ds(1024 + 8 * n, 8)],
                    sems.at[4 + len(edges)],
                )
            )
    tables = [
        pltpu.make_async_copy(pick_ref, pick_s, sems.at[8]),
        pltpu.make_async_copy(table_ref, table_s, sems.at[9]),
    ]
    for copy in parts + tables + edges:
        copy.start()
    for copy in tables:
        copy.wait()
    sub = lax.broadcasted_iota(jnp.int32, (8, 128), 0)

    def amplitude(b, carry):
        amp = jnp.zeros((8, 128), F32)
        for i in range(8):
            amp = jnp.where(sub == i, 0.1 * table_s[pick_s[0, 8 * b + i]], amp)
        amp_ref[pl.ds(pl.multiple_of(b * 8, 8), 8), :] = amp
        return carry

    lax.fori_loop(0, 16, amplitude, 0)

    def block(b, carry):
        for half, out in enumerate((ends_ref.at[0], ends_ref.at[1])):
            start = pl.multiple_of(b * 128, 8) + 8 * half
            vals = turned([x_s[pl.ds(start + 16 * i, 8), :] for i in range(8)])
            for r in range(8):
                out[pl.ds(pl.multiple_of(b * 8, 8) + 128 * r, 8), :] = vals[r]
        return carry

    for n in range(4):
        parts[n].wait()
        lax.fori_loop(4 * n, 4 * n + 4, block, 0)
    for copy in edges:
        copy.wait()
    core = lax.axis_index("core")
    cross_ref[...] = ends_ref[core]
    chip_ref[...] = ends_ref[1 - core]


def inner_kernel(
    count_ref, ends_ref, amp_ref, bits_ref,
    last_ref, prev_ref, sgt_ref, c_s, h_s, src_s, f_s,
):
    head_ref, tail_ref = ends_ref.at[0], ends_ref.at[1]
    sgt_ref[...] = (2.0 * bits_ref[0].astype(F32) - 1.0).astype(jnp.bfloat16)
    for r in range(16):
        ref, at = (head_ref, 1024 + r) if r < 8 else (tail_ref, 1016 + r)
        spread_rows(r, ref[at : at + 1, :], ref[at + 8 : at + 9, :], c_s, h_s, src_s)
    count = count_ref[0]

    def block(pair, carry):
        state = []
        for u in range(2):
            b = 2 * pair + u
            rows = pl.ds(pl.multiple_of(b * 8, 8), 8)
            amp = amp_ref[rows, :]
            old = [
                ref[pl.ds(pl.multiple_of(b * 8, 8) + 128 * r, 8), :]
                for ref in (head_ref, tail_ref)
                for r in range(8)
            ]
            for r in range(1, 15):
                f_s[u, 8 * r : 8 * r + 8, :] = amp * src_s[8 * r : 8 * r + 8, :]
            for r in (0, 15):
                last_ref[r, rows, :] = old[r]
            state.append((rows, old))
        for t in range(7):
            stepped = []
            for u, (rows, old) in enumerate(state):
                new = list(old)
                for r in range(t + 1, 15 - t):
                    at = slice(8 * r, 8 * r + 8)
                    new[r] = advance(
                        old[r], old[r - 1], old[r + 1],
                        c_s[at, :], h_s[at, :], f_s[u, at, :], t < count,
                    )
                for r in (t + 1, 14 - t):
                    prev_ref[r, rows, :] = old[r]
                    last_ref[r, rows, :] = new[r]
                stepped.append((rows, new))
            state = stepped
        return carry

    lax.fori_loop(0, 8, block, 0)


def flow_kernel(
    count_ref, last_ref, prev_ref, cross_ref, chip_ref, ends_ref, amp_ref, sgt_ref,
    field_ref, sk_ref, d0, d1, d2, d3, c_s, h_s, src_s, f_s, s_s, halo_s,
):
    core = lax.axis_index("core")
    halo_s[core] = cross_ref[...]
    halo_s[1 - core] = chip_ref[...]
    bef_ref, aft_ref = halo_s.at[0], halo_s.at[1]
    head_ref, tail_ref = ends_ref.at[0], ends_ref.at[1]
    for r in range(32):
        ref = (bef_ref, head_ref, tail_ref, aft_ref)[r // 8]
        at = 1024 + r % 8
        rate, src = ref[at : at + 1, :], ref[at + 8 : at + 9, :]
        spread_rows(r, rate, src, c_s, h_s, src_s)
    count = count_ref[0]

    def block(pair, carry):
        state = []
        for u in range(2):
            start = pl.multiple_of(pair * 16 + 8 * u, 8)
            rows = pl.ds(start, 8)
            amp = amp_ref[rows, :]
            for r in range(1, 31):
                f_s[u, 8 * r : 8 * r + 8, :] = amp * src_s[8 * r : 8 * r + 8, :]
            low = {r - 8: bef_ref[pl.ds(start + 128 * r, 8), :] for r in range(8)}
            high = {r + 16: aft_ref[pl.ds(start + 128 * r, 8), :] for r in range(8)}
            state.append((rows, low, high))
        for t in range(STEPS):
            stepped = []
            for u, (rows, low, high) in enumerate(state):
                low[t] = last_ref[t, rows, :]
                high[15 - t] = last_ref[15 - t, rows, :]
                low[t + 1] = last_ref[8, rows, :] if t == 7 else prev_ref[t + 1, rows, :]
                high[14 - t] = last_ref[7, rows, :] if t == 7 else prev_ref[14 - t, rows, :]
                sides = []
                for old, first in ((low, t - 7), (high, 15 - t)):
                    new = {}
                    for r in range(first, first + 8):
                        at = slice(8 * r + 64, 8 * r + 72)
                        new[r] = advance(
                            old[r], old[r - 1], old[r + 1],
                            c_s[at, :], h_s[at, :], f_s[u, at, :], t < count,
                        )
                    sides.append(new)
                stepped.append((rows, *sides))
            state = stepped
        for rows, low, high in state:
            for r in range(8):
                field_ref[r, rows, :] = low[r]
                field_ref[8 + r, rows, :] = high[8 + r]
        return carry

    lax.fori_loop(0, 8, block, 0)
    signs_t = sgt_ref[...]
    for q in range(4):
        parts = []
        for i in range(4):
            sk = signs_mm(signs_t, field_ref[4 * q + i])
            sk_ref[4 * q + i] = sk
            parts.append(sk)
        parts = exchange_blocks(exchange_blocks(parts, 1, 8), 2, 16)
        for j in range(4):
            s_s[j, q] = parts[j]
    place = lax.axis_index("y")
    for d, out in enumerate((d0, d1, d2, d3)):
        out[...] = s_s[rest_of(place, d)]


def leaf_sum_kernel(field_ref, sk_ref, bits_ref, yt_ref, sg_ref, sgt_ref):
    for level in range(5):
        signs = 2.0 * bits_ref[level].astype(F32) - 1.0
        sg_ref[level] = signs.T.astype(jnp.bfloat16)
        sgt_ref[level] = signs.astype(jnp.bfloat16)
    yt = jnp.zeros((64, 128), F32)
    for r in range(16):
        yt = yt + mm_nt(sk_ref[r], field_ref[r])
    yt_ref[...] = yt


def cross_kernel(yt_ref, r0, r1, r2, r3, keep_ref, send_ref, all_s, z_s, pay_s):
    place = lax.axis_index("y")
    for d, ref in enumerate((r0, r1, r2, r3)):
        all_s[rest_of(place, -d)] = ref[...]
    slabs = [jnp.zeros((64, 128), F32)] * 3
    for q in range(4):
        s0, s1, s2, s3 = (all_s[g, q] for g in range(4))
        upper = jnp.concatenate([s2, s3], axis=0)
        first = mm_nt(s0, jnp.concatenate([s1, s3], axis=0))
        slabs[1] = slabs[1] + mm_nt(s0, upper)
        slabs[2] = slabs[2] + mm_nt(s1, upper)
        slabs[0] = slabs[0] + jnp.concatenate([first[:, :64], mm_nt(s2, s3)], axis=1)
    for n in range(3):
        z_s[64 * n : 64 * n + 64] = slabs[n]
    for c in range(2):
        pay_s[c, 0:32] = yt_ref[32 * c : 32 * c + 32]
        for d in range(4):
            at = pl.multiple_of(48 * rest_of(place, d) + 24 * c, 8)
            pay_s[c, 32 + 24 * d : 56 + 24 * d] = z_s[pl.ds(at, 24), :]
    core = lax.axis_index("core")
    keep_ref[...] = pay_s[core]
    send_ref[...] = pay_s[1 - core]


def leaf_kernel(own_ref, other_ref, sg_ref, sgt_ref, out_ref):
    low, high = both_halves(own_ref, other_ref)
    signs, _ = signs_of((sg_ref, sgt_ref), 0)
    (b,), (moment,) = compress([jnp.concatenate([low[:32], high[:32]], axis=0)], signs)
    out_ref[0:64] = jnp.concatenate([b, gram_of(b, moment)], axis=1)
    out_ref[64:88] = low[32:]
    out_ref[88:112] = high[32:]


def middle_kernel(p0, p1, p2, p3, all_ref, sg_ref, sgt_ref, out_ref, pay_s, z_s):
    place = lax.axis_index("y")
    for d, ref in enumerate((p0, p1, p2, p3)):
        pay_s[rest_of(place, -d)] = ref[...]
    for g in range(4):
        z_s[48 * g : 48 * g + 48] = pay_s[g, 64:112]
    bs = [pay_s[g, 0:64][:, :64] for g in range(4)]
    grams = [pay_s[g, 0:64][:, 64:] for g in range(4)]
    inside = z_s[0:64]
    crosses = [mm_nt(mm(bs[0], inside[:, :64]), bs[1]), mm_nt(mm(bs[2], inside[:, 64:]), bs[3])]
    signs, signs_t = signs_of((sg_ref, sgt_ref), 1)
    yts = [
        sketch_of_pair(grams[2 * n], crosses[n], grams[2 * n + 1], signs_t) for n in range(2)
    ]
    ups, moments = compress(yts, signs)
    half = 0.5**0.5
    ws = []
    for n in range(2):
        low = signs_mm(signs_t[:, :64], bs[2 * n])
        high = signs_mm(signs_t[:, 64:], bs[2 * n + 1])
        ws.append(mm(ups[n], jnp.concatenate([low, high], axis=1)) * half)
    cross = mm_nt(mm(ws[0], z_s[64:192]), ws[1])
    signs, signs_t = signs_of((sg_ref, sgt_ref), 2)
    first, second = (gram_of(u, m) for u, m in zip(ups, moments))
    (b,), (moment,) = compress([sketch_of_pair(first, cross, second, signs_t)], signs)
    low = signs_mm(signs_t[:, :64], ws[0])
    high = signs_mm(signs_t[:, 64:], ws[1])
    w = mm(b, jnp.concatenate([low, high], axis=1)) * half
    for q in range(4):
        out_ref[64 * q : 64 * q + 64] = mm(
            w, jnp.concatenate([all_ref[g, q] for g in range(4)], axis=0)
        )
    gram = gram_of(b, moment)
    out_ref[256:288] = jnp.concatenate([gram[:32], gram[32:]], axis=1)


def upper_kernel(r0, r1, r2, r3, sg_ref, sgt_ref, s_ref, keep_ref, send_ref, all_s, pay_s):
    place = lax.axis_index("x")
    for d, ref in enumerate((r0, r1, r2, r3)):
        all_s[rest_of(place, -d)] = ref[0:256]
    _, signs_t = signs_of((sg_ref, sgt_ref), 3)
    slabs = [jnp.zeros((64, 64), F32)] * 3
    for q in range(4):
        at = slice(64 * q, 64 * q + 64)
        sks = []
        for n in range(2):
            low, high = all_s[2 * n, at], all_s[2 * n + 1, at]
            sk = signs_mm(signs_t, jnp.concatenate([low, high], axis=0)) * (0.5**0.5)
            s_ref[n, q] = sk
            sks.append(sk)
            slabs[n] = slabs[n] + mm_nt(low, high)
        slabs[2] = slabs[2] + mm_nt(*sks)
    for c in range(2):
        at = slice(32 * c, 32 * c + 32)
        pay_s[c, 0:32] = jnp.concatenate([slabs[0][at], slabs[1][at]], axis=1)
        pay_s[c, 32:48] = jnp.concatenate(
            [slabs[2][32 * c : 32 * c + 16], slabs[2][32 * c + 16 : 32 * c + 32]], axis=1
        )
    core = lax.axis_index("core")
    keep_ref[...] = pay_s[core]
    send_ref[...] = pay_s[1 - core]


def last_kernel(own_ref, other_ref, r0, r1, r2, r3, s_ref, sg_ref, sgt_ref, out_ref, gram_s):
    place = lax.axis_index("x")
    for d, ref in enumerate((r0, r1, r2, r3)):
        gram_s[rest_of(place, -d)] = ref[256:288]
    grams = []
    for g in range(4):
        packed = gram_s[g]
        grams.append(jnp.concatenate([packed[:, :64], packed[:, 64:]], axis=0))
    low, high = both_halves(own_ref, other_ref)
    pairs = jnp.concatenate([low[:32], high[:32]], axis=0)
    inside = jnp.concatenate(
        [low[32:, :64], low[32:, 64:], high[32:, :64], high[32:, 64:]], axis=0
    )
    signs, signs_t = signs_of((sg_ref, sgt_ref), 3)
    yts = [
        sketch_of_pair(grams[2 * n], pairs[:, 64 * n : 64 * n + 64], grams[2 * n + 1], signs_t)
        for n in range(2)
    ]
    bs, moments = compress(yts, signs)
    cross = mm_nt(mm(bs[0], inside), bs[1])
    first, second = (gram_of(u, m) for u, m in zip(bs, moments))
    signs, signs_t = signs_of((sg_ref, sgt_ref), 4)
    (b,), _ = compress([sketch_of_pair(first, cross, second, signs_t)], signs)
    lower = signs_mm(signs_t[:, :64], bs[0])
    upper = signs_mm(signs_t[:, 64:], bs[1])
    w = mm(b, jnp.concatenate([lower, upper], axis=1)) * (0.5**0.5)
    lane = lax.broadcasted_iota(jnp.int32, (128, 128), 1)
    block = lax.shift_right_logical(lane, 5)
    mine = jnp.zeros((128, 128), F32)
    for q in range(4):
        own = jnp.concatenate([s_ref[0, q], s_ref[1, q]], axis=0)
        turned = pltpu.roll(own, lax.rem(32 * q - 32 * place + 128, 128), 1)
        mine = jnp.where(block == q, turned, mine)
    out_ref[...] = mm(w, mine)


def call(kernel, out_shapes, smem, *args, scratch=(), limit=16, cost=None):
    specs = [SMEM] * smem + [VMEM] * (len(args) - smem)
    return pl.pallas_call(
        kernel,
        out_shape=out_shapes,
        in_specs=specs,
        out_specs=jax.tree.map(lambda _: VMEM, out_shapes),
        scratch_shapes=list(scratch),
        cost_estimate=cost,
        compiler_params=pltpu.CompilerParams(vmem_limit_bytes=limit << 20),
    )(*args)


def in_hbm(value):
    return pltpu.with_memory_space_constraint(value, pltpu.HBM)


def shape(*dims):
    return jax.ShapeDtypeStruct(dims, F32)


def shift(value, axis, by):
    n = lax.axis_size(axis)
    return lax.ppermute(value, axis, [(i, (i + by) % n) for i in range(n)])


def from_ring(value, axis):
    return [value] + [shift(value, axis, d) for d in (1, 2, 3)]


def total(parts):
    return (parts[0] + parts[1]) + (parts[2] + parts[3])


def sum_over(value, axis):
    peers = lax.axis_size(axis)
    sent = jnp.broadcast_to(value[None], (peers, *value.shape))
    return lax.all_to_all(sent, axis, 0, 0, tiled=True).sum(axis=0)


def per_device(init_state, coef, source, amplitudes, sample_idx, step_counts, sketch_signs):
    field = init_state[0]
    rate = coef[0]
    slabs = ("z", "core")
    n = lax.axis_size(slabs)
    between = [(i, i + 1) for i in range(1, n - 1, 2)] + [(i, i - 1) for i in range(2, n, 2)]
    ends, cross, chip, amp = pl.pallas_call(
        pack_kernel,
        out_shape=(shape(2, 1040, 128), shape(1040, 128), shape(1040, 128), shape(128, 128)),
        in_specs=[pl.BlockSpec(memory_space=pltpu.HBM)] * 5,
        out_specs=(VMEM,) * 4,
        scratch_shapes=[
            pltpu.VMEM((2048, 128), F32),
            pltpu.SMEM((1, 128), jnp.int32),
            pltpu.SMEM((64,), F32),
            pltpu.SemaphoreType.DMA((10,)),
        ],
        compiler_params=pltpu.CompilerParams(vmem_limit_bytes=16 << 20),
    )(
        *(
            in_hbm(v)
            for v in (field.reshape(2048, 128), rate, source, sample_idx, amplitudes)
        )
    )
    bits = jnp.swapaxes(sketch_signs, 1, 2)
    cross = lax.ppermute(cross, slabs, between)
    chip = shift(chip, "core", 1)
    last, prev, first_signs = call(
        inner_kernel,
        (
            shape(16, 128, 128),
            shape(16, 128, 128),
            jax.ShapeDtypeStruct((64, 128), jnp.bfloat16),
        ),
        1,
        step_counts,
        ends,
        amp,
        bits,
        scratch=[pltpu.VMEM((128, 128), F32)] * 3 + [pltpu.VMEM((2, 128, 128), F32)],
        cost=pl.CostEstimate(flops=4_000_000_000, bytes_accessed=4_000_000, transcendentals=0),
    )
    final, sks, *chunks = call(
        flow_kernel,
        (shape(16, 128, 128), shape(16, 64, 128)) + (shape(4, 64, 128),) * 4,
        1,
        step_counts,
        last,
        prev,
        cross,
        chip,
        ends,
        amp,
        first_signs,
        scratch=[pltpu.VMEM((256, 128), F32)] * 3
        + [
            pltpu.VMEM((2, 256, 128), F32),
            pltpu.VMEM((4, 4, 64, 128), F32),
            pltpu.VMEM((2, 1040, 128), F32),
        ],
    )
    yt, signs, signs_t = call(
        leaf_sum_kernel,
        (
            shape(64, 128),
            jax.ShapeDtypeStruct((5, 128, 64), jnp.bfloat16),
            jax.ShapeDtypeStruct((5, 64, 128), jnp.bfloat16),
        ),
        0,
        final,
        sks,
        bits,
        cost=pl.CostEstimate(flops=2_000_000_000, bytes_accessed=2_000_000, transcendentals=0),
    )
    got = [chunks[0]] + [shift(chunks[d], "y", d) for d in (1, 2, 3)]
    keep, send, sketches = call(
        cross_kernel,
        (shape(128, 128), shape(128, 128), shape(4, 4, 64, 128)),
        0,
        yt,
        *got,
        scratch=[pltpu.VMEM((192, 128), F32), pltpu.VMEM((2, 128, 128), F32)],
    )
    half = keep + shift(send, "core", 1)
    quarters = [half[32:56]] + [shift(half[32 + 24 * d : 56 + 24 * d], "y", d) for d in (1, 2, 3)]
    own = sum_over(jnp.concatenate([half[:32], total(quarters)], axis=0), "z")
    leaf = call(leaf_kernel, shape(112, 128), 0, own, shift(own, "core", 1), signs, signs_t)
    piece = call(
        middle_kernel,
        shape(288, 128),
        0,
        *from_ring(leaf, "y"),
        sketches,
        signs,
        signs_t,
        scratch=[pltpu.VMEM((4, 112, 128), F32), pltpu.VMEM((192, 128), F32)],
    )
    pieces = from_ring(piece, "x")
    s, keep, send = call(
        upper_kernel,
        (shape(2, 4, 64, 128), shape(48, 128), shape(48, 128)),
        0,
        *pieces,
        signs,
        signs_t,
        scratch=[pltpu.VMEM((4, 256, 128), F32), pltpu.VMEM((2, 48, 128), F32)],
    )
    half = keep + shift(send, "core", 1)
    own = sum_over(total(from_ring(half, "y")), "z")
    out = call(
        last_kernel,
        shape(64, 128),
        0,
        own,
        shift(own, "core", 1),
        *pieces,
        s,
        signs,
        signs_t,
        scratch=[pltpu.VMEM((4, 32, 128), F32)],
    )
    return out.reshape(64, 16, 8)


def solution(mesh):
    fine = Mesh(mesh.devices.reshape(4, 4, 8, 2), ("x", "y", "z", "core"))
    group, slab = ("x", "y"), ("z", "core")
    return jax.shard_map(
        per_device,
        mesh=fine,
        in_specs=(
            P(group, None, slab, None),
            P(group, slab, None),
            P(slab, None),
            P(),
            P(group, None),
            P(group),
            P(),
        ),
        out_specs=P(None, slab, group),
        check_vma=False,
    )
```

```python
import functools
import math

import jax
import jax.numpy as jnp
from jax import lax
from jax.experimental import pallas as pl
from jax.experimental.pallas import tpu as pltpu
from jax.sharding import Mesh
from jax.sharding import PartitionSpec as P

STEPS = 8
SCALE = 1.0 / math.sqrt(128.0)
HI = lax.Precision.HIGHEST
F32 = jnp.float32
VMEM = pl.BlockSpec(memory_space=pltpu.VMEM)
SMEM = pl.BlockSpec(memory_space=pltpu.SMEM)


def mm(a, b):
    return lax.dot_general(
        a, b, (((1,), (0,)), ((), ())), precision=HI, preferred_element_type=F32
    )


def mm_nt(a, b):
    return lax.dot_general(
        a, b, (((1,), (1,)), ((), ())), precision=HI, preferred_element_type=F32
    )


def thirds(x):
    hi = x.astype(jnp.bfloat16)
    rest = x - hi.astype(F32)
    mid = rest.astype(jnp.bfloat16)
    return hi, mid, (rest - mid.astype(F32)).astype(jnp.bfloat16)


def signs_mm(signs, x):
    hi, mid, lo = (jnp.dot(signs, t, preferred_element_type=F32) for t in thirds(x))
    return (hi + (mid + lo)) * SCALE


def mm_signs(x, signs):
    hi, mid, lo = (jnp.dot(t, signs, preferred_element_type=F32) for t in thirds(x))
    return (hi + (mid + lo)) * SCALE


def product(a, b):
    (ah, am, _), (bh, bm, _) = thirds(a), thirds(b)
    left = jnp.concatenate([ah, am], axis=0)
    high = jnp.dot(left, bh, preferred_element_type=F32)
    low = jnp.dot(left, bm, preferred_element_type=F32)
    rows = a.shape[0]
    return high[:rows] + (high[rows:] + low[:rows]) + low[rows:]


def halves(x):
    hi = x.astype(jnp.bfloat16)
    mid = (x - hi.astype(F32)).astype(jnp.bfloat16)
    return jnp.concatenate([hi, mid], axis=1), jnp.concatenate([mid, hi], axis=1)


def inner_products(left, right):
    dims = (((1,), (1,)), ((), ()))
    same = lax.dot_general(left[0], right[0], dims, preferred_element_type=F32)
    return same + lax.dot_general(left[0], right[1], dims, preferred_element_type=F32)


def stacked(first, second):
    return tuple(jnp.concatenate([a, b], axis=0) for a, b in zip(first, second))


def rows_of(v, i):
    return jnp.broadcast_to(v[i : i + 1, :], v.shape)


def factor(blocks, split):
    work = list(blocks)
    shape_of = work[0].shape
    sub = lax.broadcasted_iota(jnp.int32, shape_of, 0)
    lane = lax.broadcasted_iota(jnp.int32, shape_of, 1)
    base = jnp.where(lane < 64, 0, 64) if split else jnp.zeros(shape_of, jnp.int32)
    done = []
    for kb in range(8):
        cols = []
        for j in range(8):
            index = base + (8 * kb + j)
            cols.append([jnp.take_along_axis(work[i], index, axis=1) for i in range(kb, 8)])
        rows = [rows_of(work[kb], j) for j in range(8)]
        el = [[rows_of(cols[j][0], i) if i <= j else None for j in range(8)] for i in range(8)]
        outs, scaled = [], []
        for p in range(0, 8, 2):
            q = p + 1
            a, b, c = el[p][p], el[p][q], el[q][q]
            det = a * c - b * b
            inv = 1.0 / det
            rp, rq = rows[p], rows[q]
            root = lax.rsqrt(a)
            outs += [rp * root, (a * rq - b * rp) * (root * lax.rsqrt(det))]
            off = b * inv
            scaled += [(c * inv) * rp - off * rq, (a * inv) * rq - off * rp]
            left = {j: c * el[p][j] - b * el[q][j] for j in range(q + 1, 8)}
            right = {j: a * el[q][j] - b * el[p][j] for j in range(q + 1, 8)}
            for j in range(q + 1, 8):
                x, y = left[j] * inv, right[j] * inv
                for i in range(q + 1, j + 1):
                    el[i][j] = el[i][j] - (el[p][i] * left[j] + el[q][i] * right[j]) * inv
                rows[j] = rows[j] - (x * rp + y * rq)
                for n in range(1, 8 - kb):
                    cols[j][n] = cols[j][n] - (cols[p][n] * x + cols[q][n] * y)
        out = outs[0]
        for p in range(1, 8):
            out = jnp.where(sub == p, outs[p], out)
        done.append(out)
        for i in range(kb + 1, 8):
            acc = [cols[p][i - kb] * scaled[p] for p in range(8)]
            while len(acc) > 1:
                acc = [acc[2 * t] + acc[2 * t + 1] for t in range(len(acc) // 2)]
            work[i] = work[i] - acc[0]
    return jnp.concatenate(done, axis=0)


def shift_of(mat, diag):
    trace = jnp.sum(jnp.where(diag, mat, 0.0), keepdims=True)
    return jnp.where(diag, trace * (0.0001 / 64.0), 0.0)


def row_blocks(mat):
    return [mat[8 * i : 8 * i + 8] for i in range(8)]


def compress(yts, signs):
    row = lax.broadcasted_iota(jnp.int32, (64, 128), 0)
    lane = lax.broadcasted_iota(jnp.int32, (64, 128), 1)
    diag = lane == row
    wide = jnp.concatenate([signs, jnp.zeros((128, 64), jnp.bfloat16)], axis=1)
    moments = [mm_signs(yt, wide) for yt in yts]
    firsts = [
        factor(row_blocks(jnp.where(lane == row + 64, 1.0, m + shift_of(m, diag))), False)
        for m in moments
    ]
    linvs = [f[:, 64:] for f in firsts]
    hs = [mm(li, yt) for li, yt in zip(linvs, yts)]
    if len(hs) == 1:
        pad = jnp.zeros((64, 128), F32)
        inner = mm_nt(hs[0], jnp.concatenate([hs[0], pad], axis=0))
        inner = inner + shift_of(inner, diag)
        second = factor(row_blocks(inner), False)
        kts = [jnp.where(lane >= row, second, 0.0)[:, :64]]
    else:
        small = [mm_nt(h, h) for h in hs]
        small = [c + shift_of(c, diag[:, :64]) for c in small]
        second = factor(row_blocks(jnp.concatenate(small, axis=1)), True)
        second = jnp.where((lane & 63) >= row, second, 0.0)
        kts = [second[:, :64], second[:, 64:]]
    return [mm(k, li) for k, li in zip(kts, linvs)], [m[:, :64] for m in moments]


def gram_of(b, moment):
    return mm_nt(mm(b, moment), b)


def sketch_of_pair(first, cross, second, signs_t):
    top = jnp.concatenate([first, cross], axis=1)
    bottom = jnp.concatenate([cross.T, second], axis=1)
    return 0.5 * signs_mm(signs_t, jnp.concatenate([top, bottom], axis=0))


def signs_of(signs_refs, level):
    return signs_refs[0][level], signs_refs[1][level]


def both_halves(own_ref, other_ref):
    first = lax.axis_index("core") == 0
    own = own_ref[...]
    other = other_ref[...]
    return jnp.where(first, own, other), jnp.where(first, other, own)


def rest_of(value, by):
    return lax.rem(value + (by + 4), 4)


def exchange_blocks(vals, bit, lane_bit):
    lane = lax.broadcasted_iota(jnp.int32, vals[0].shape, 1)
    low = (lane & lane_bit) == 0
    out = list(vals)
    for i in range(len(vals)):
        if i & bit:
            continue
        a, b = vals[i], vals[i | bit]
        out[i] = jnp.where(low, a, pltpu.roll(b, lane_bit, 1))
        out[i | bit] = jnp.where(low, pltpu.roll(a, 128 - lane_bit, 1), b)
    return out


def advance(mid, above, below, rate, bend_rate, force, live):
    lane = lax.broadcasted_iota(jnp.int32, mid.shape, 1)
    left = jnp.where(lane != 0, pltpu.roll(mid, 1, 1), 0.0)
    right = jnp.where(lane != 127, pltpu.roll(mid, 127, 1), 0.0)
    lap = (below + above) + (right + left) - 4.0 * mid
    bend = jnp.tanh(mid)
    return jnp.where(live, mid + (rate + bend_rate * (bend * bend)) * lap + force, mid)


def spread_rows(at, rate, src, c_s, h_s, src_s):
    at = slice(8 * at, 8 * at + 8)
    c_s[at, :] = jnp.broadcast_to(rate, (8, 128))
    h_s[at, :] = jnp.broadcast_to(0.5 * rate, (8, 128))
    src_s[at, :] = jnp.broadcast_to(src, (8, 128))


def turned(vals):
    sub = lax.broadcasted_iota(jnp.int32, vals[0].shape, 0)
    out = list(vals)
    for bit in (1, 2, 4):
        low = (sub & bit) == 0
        for i in range(8):
            if i & bit:
                continue
            a, b = out[i], out[i | bit]
            out[i] = jnp.where(low, a, pltpu.roll(b, bit, 0))
            out[i | bit] = jnp.where(low, pltpu.roll(a, 8 - bit, 0), b)
    return out


def pack_kernel(
    x_ref, rate_ref, src_ref, pick_ref, table_ref,
    ends_ref, cross_ref, chip_ref, amp_ref, x_s, pick_s, table_s, sems,
):
    parts = [
        pltpu.make_async_copy(
            x_ref.at[pl.ds(512 * n, 512)], x_s.at[pl.ds(512 * n, 512)], sems.at[n]
        )
        for n in range(4)
    ]
    edges = []
    for half, out in enumerate((ends_ref.at[0], ends_ref.at[1])):
        for n, ref in enumerate((rate_ref, src_ref)):
            edges.append(
                pltpu.make_async_copy(
                    ref.at[pl.ds(8 * half, 8)],
                    out.at[pl.ds(1024 + 8 * n, 8)],
                    sems.at[4 + len(edges)],
                )
            )
    tables = [
        pltpu.make_async_copy(pick_ref, pick_s, sems.at[8]),
        pltpu.make_async_copy(table_ref, table_s, sems.at[9]),
    ]
    for copy in parts + tables + edges:
        copy.start()
    for copy in tables:
        copy.wait()
    sub = lax.broadcasted_iota(jnp.int32, (8, 128), 0)

    def amplitude(b, carry):
        amp = jnp.zeros((8, 128), F32)
        for i in range(8):
            amp = jnp.where(sub == i, 0.1 * table_s[pick_s[0, 8 * b + i]], amp)
        amp_ref[pl.ds(pl.multiple_of(b * 8, 8), 8), :] = amp
        return carry

    lax.fori_loop(0, 16, amplitude, 0)

    def block(b, carry):
        for half, out in enumerate((ends_ref.at[0], ends_ref.at[1])):
            start = pl.multiple_of(b * 128, 8) + 8 * half
            vals = turned([x_s[pl.ds(start + 16 * i, 8), :] for i in range(8)])
            for r in range(8):
                out[pl.ds(pl.multiple_of(b * 8, 8) + 128 * r, 8), :] = vals[r]
        return carry

    for n in range(4):
        parts[n].wait()
        lax.fori_loop(4 * n, 4 * n + 4, block, 0)
    for copy in edges:
        copy.wait()
    core = lax.axis_index("core")
    cross_ref[...] = ends_ref[core]
    chip_ref[...] = ends_ref[1 - core]


def inner_kernel(
    count_ref, ends_ref, amp_ref, bits_ref,
    last_ref, prev_ref, sgt_ref, c_s, h_s, src_s, f_s,
):
    head_ref, tail_ref = ends_ref.at[0], ends_ref.at[1]
    sgt_ref[...] = (2.0 * bits_ref[0].astype(F32) - 1.0).astype(jnp.bfloat16)
    for r in range(16):
        ref, at = (head_ref, 1024 + r) if r < 8 else (tail_ref, 1016 + r)
        spread_rows(r, ref[at : at + 1, :], ref[at + 8 : at + 9, :], c_s, h_s, src_s)
    count = count_ref[0]

    def block(pair, carry):
        state = []
        for u in range(2):
            b = 2 * pair + u
            rows = pl.ds(pl.multiple_of(b * 8, 8), 8)
            amp = amp_ref[rows, :]
            old = [
                ref[pl.ds(pl.multiple_of(b * 8, 8) + 128 * r, 8), :]
                for ref in (head_ref, tail_ref)
                for r in range(8)
            ]
            for r in range(1, 15):
                f_s[u, 8 * r : 8 * r + 8, :] = amp * src_s[8 * r : 8 * r + 8, :]
            for r in (0, 15):
                last_ref[r, rows, :] = old[r]
            state.append((rows, old))
        for t in range(7):
            stepped = []
            for u, (rows, old) in enumerate(state):
                new = list(old)
                for r in range(t + 1, 15 - t):
                    at = slice(8 * r, 8 * r + 8)
                    new[r] = advance(
                        old[r], old[r - 1], old[r + 1],
                        c_s[at, :], h_s[at, :], f_s[u, at, :], t < count,
                    )
                for r in (t + 1, 14 - t):
                    prev_ref[r, rows, :] = old[r]
                    last_ref[r, rows, :] = new[r]
                stepped.append((rows, new))
            state = stepped
        return carry

    lax.fori_loop(0, 8, block, 0)


def flow_kernel(
    count_ref, last_ref, prev_ref, cross_ref, chip_ref, ends_ref, amp_ref, sgt_ref,
    field_ref, sk_ref, d0, d1, d2, d3, c_s, h_s, src_s, f_s, s_s, halo_s,
):
    core = lax.axis_index("core")
    halo_s[core] = cross_ref[...]
    halo_s[1 - core] = chip_ref[...]
    bef_ref, aft_ref = halo_s.at[0], halo_s.at[1]
    head_ref, tail_ref = ends_ref.at[0], ends_ref.at[1]
    for r in range(32):
        ref = (bef_ref, head_ref, tail_ref, aft_ref)[r // 8]
        at = 1024 + r % 8
        rate, src = ref[at : at + 1, :], ref[at + 8 : at + 9, :]
        spread_rows(r, rate, src, c_s, h_s, src_s)
    count = count_ref[0]

    def block(pair, carry):
        state = []
        for u in range(2):
            start = pl.multiple_of(pair * 16 + 8 * u, 8)
            rows = pl.ds(start, 8)
            amp = amp_ref[rows, :]
            for r in range(1, 31):
                f_s[u, 8 * r : 8 * r + 8, :] = amp * src_s[8 * r : 8 * r + 8, :]
            low = {r - 8: bef_ref[pl.ds(start + 128 * r, 8), :] for r in range(8)}
            high = {r + 16: aft_ref[pl.ds(start + 128 * r, 8), :] for r in range(8)}
            state.append((rows, low, high))
        for t in range(STEPS):
            stepped = []
            for u, (rows, low, high) in enumerate(state):
                low[t] = last_ref[t, rows, :]
                high[15 - t] = last_ref[15 - t, rows, :]
                low[t + 1] = last_ref[8, rows, :] if t == 7 else prev_ref[t + 1, rows, :]
                high[14 - t] = last_ref[7, rows, :] if t == 7 else prev_ref[14 - t, rows, :]
                sides = []
                for old, first in ((low, t - 7), (high, 15 - t)):
                    new = {}
                    for r in range(first, first + 8):
                        at = slice(8 * r + 64, 8 * r + 72)
                        new[r] = advance(
                            old[r], old[r - 1], old[r + 1],
                            c_s[at, :], h_s[at, :], f_s[u, at, :], t < count,
                        )
                    sides.append(new)
                stepped.append((rows, *sides))
            state = stepped
        for rows, low, high in state:
            for r in range(8):
                field_ref[r, rows, :] = low[r]
                field_ref[8 + r, rows, :] = high[8 + r]
        return carry

    lax.fori_loop(0, 8, block, 0)
    signs_t = sgt_ref[...]
    for q in range(4):
        parts = []
        for i in range(4):
            sk = signs_mm(signs_t, field_ref[4 * q + i])
            sk_ref[4 * q + i] = sk
            parts.append(sk)
        parts = exchange_blocks(exchange_blocks(parts, 1, 8), 2, 16)
        for j in range(4):
            s_s[j, q] = parts[j]
    place = lax.axis_index("y")
    for d, out in enumerate((d0, d1, d2, d3)):
        out[...] = s_s[rest_of(place, d)]


def leaf_sum_kernel(field_ref, sk_ref, bits_ref, yt_ref, sg_ref, sgt_ref):
    for level in range(5):
        signs = 2.0 * bits_ref[level].astype(F32) - 1.0
        sg_ref[level] = signs.T.astype(jnp.bfloat16)
        sgt_ref[level] = signs.astype(jnp.bfloat16)
    yt = jnp.zeros((64, 128), F32)
    for r in range(16):
        yt = yt + mm_nt(sk_ref[r], field_ref[r])
    yt_ref[...] = yt


def cross_kernel(yt_ref, r0, r1, r2, r3, keep_ref, send_ref, all_s, z_s, pay_s):
    place = lax.axis_index("y")
    for d, ref in enumerate((r0, r1, r2, r3)):
        all_s[rest_of(place, -d)] = ref[...]
    slabs = [jnp.zeros((64, 128), F32)] * 3
    for q in range(4):
        s0, s1, s2, s3 = (halves(all_s[g, q]) for g in range(4))
        upper = stacked(s2, s3)
        slabs[1] = slabs[1] + inner_products(s0, upper)
        slabs[2] = slabs[2] + inner_products(s1, upper)
        first, second = inner_products(s0, s1), inner_products(s2, s3)
        slabs[0] = slabs[0] + jnp.concatenate([first, second], axis=1)
    for n in range(3):
        z_s[64 * n : 64 * n + 64] = slabs[n]
    for c in range(2):
        pay_s[c, 0:32] = yt_ref[32 * c : 32 * c + 32]
        for d in range(4):
            at = pl.multiple_of(48 * rest_of(place, d) + 24 * c, 8)
            pay_s[c, 32 + 24 * d : 56 + 24 * d] = z_s[pl.ds(at, 24), :]
    core = lax.axis_index("core")
    keep_ref[...] = pay_s[core]
    send_ref[...] = pay_s[1 - core]


def leaf_kernel(own_ref, other_ref, sg_ref, sgt_ref, out_ref):
    low, high = both_halves(own_ref, other_ref)
    signs, _ = signs_of((sg_ref, sgt_ref), 0)
    (b,), (moment,) = compress([jnp.concatenate([low[:32], high[:32]], axis=0)], signs)
    out_ref[0:64] = jnp.concatenate([b, gram_of(b, moment)], axis=1)
    out_ref[64:88] = low[32:]
    out_ref[88:112] = high[32:]


def middle_kernel(p0, p1, p2, p3, all_ref, sg_ref, sgt_ref, out_ref, pay_s, z_s):
    place = lax.axis_index("y")
    for d, ref in enumerate((p0, p1, p2, p3)):
        pay_s[rest_of(place, -d)] = ref[...]
    for g in range(4):
        z_s[48 * g : 48 * g + 48] = pay_s[g, 64:112]
    bs = [pay_s[g, 0:64][:, :64] for g in range(4)]
    grams = [pay_s[g, 0:64][:, 64:] for g in range(4)]
    inside = z_s[0:64]
    crosses = [mm_nt(mm(bs[0], inside[:, :64]), bs[1]), mm_nt(mm(bs[2], inside[:, 64:]), bs[3])]
    signs, signs_t = signs_of((sg_ref, sgt_ref), 1)
    yts = [
        sketch_of_pair(grams[2 * n], crosses[n], grams[2 * n + 1], signs_t) for n in range(2)
    ]
    ups, moments = compress(yts, signs)
    half = 0.5**0.5
    ws = []
    for n in range(2):
        low = signs_mm(signs_t[:, :64], bs[2 * n])
        high = signs_mm(signs_t[:, 64:], bs[2 * n + 1])
        ws.append(mm(ups[n], jnp.concatenate([low, high], axis=1)) * half)
    cross = mm_nt(mm(ws[0], z_s[64:192]), ws[1])
    signs, signs_t = signs_of((sg_ref, sgt_ref), 2)
    first, second = (gram_of(u, m) for u, m in zip(ups, moments))
    (b,), (moment,) = compress([sketch_of_pair(first, cross, second, signs_t)], signs)
    low = signs_mm(signs_t[:, :64], ws[0])
    high = signs_mm(signs_t[:, 64:], ws[1])
    w = mm(b, jnp.concatenate([low, high], axis=1)) * half
    for q in range(4):
        own = jnp.concatenate([all_ref[g, q] for g in range(4)], axis=0)
        out_ref[64 * q : 64 * q + 64] = product(w, own)
    gram = gram_of(b, moment)
    out_ref[256:288] = jnp.concatenate([gram[:32], gram[32:]], axis=1)


def upper_kernel(r0, r1, r2, r3, sg_ref, sgt_ref, s_ref, keep_ref, send_ref, all_s, pay_s):
    place = lax.axis_index("x")
    for d, ref in enumerate((r0, r1, r2, r3)):
        all_s[rest_of(place, -d)] = ref[0:256]
    _, signs_t = signs_of((sg_ref, sgt_ref), 3)
    slabs = [jnp.zeros((64, 64), F32)] * 3
    for q in range(4):
        at = slice(64 * q, 64 * q + 64)
        sks = []
        for n in range(2):
            low, high = all_s[2 * n, at], all_s[2 * n + 1, at]
            sk = signs_mm(signs_t, jnp.concatenate([low, high], axis=0)) * (0.5**0.5)
            s_ref[n, q] = sk
            sks.append(sk)
            slabs[n] = slabs[n] + inner_products(halves(low), halves(high))
        slabs[2] = slabs[2] + inner_products(halves(sks[0]), halves(sks[1]))
    for c in range(2):
        at = slice(32 * c, 32 * c + 32)
        pay_s[c, 0:32] = jnp.concatenate([slabs[0][at], slabs[1][at]], axis=1)
        pay_s[c, 32:48] = jnp.concatenate(
            [slabs[2][32 * c : 32 * c + 16], slabs[2][32 * c + 16 : 32 * c + 32]], axis=1
        )
    core = lax.axis_index("core")
    keep_ref[...] = pay_s[core]
    send_ref[...] = pay_s[1 - core]


def last_kernel(own_ref, other_ref, r0, r1, r2, r3, s_ref, sg_ref, sgt_ref, out_ref, gram_s):
    place = lax.axis_index("x")
    for d, ref in enumerate((r0, r1, r2, r3)):
        gram_s[rest_of(place, -d)] = ref[256:288]
    grams = []
    for g in range(4):
        packed = gram_s[g]
        grams.append(jnp.concatenate([packed[:, :64], packed[:, 64:]], axis=0))
    low, high = both_halves(own_ref, other_ref)
    pairs = jnp.concatenate([low[:32], high[:32]], axis=0)
    inside = jnp.concatenate(
        [low[32:, :64], low[32:, 64:], high[32:, :64], high[32:, 64:]], axis=0
    )
    signs, signs_t = signs_of((sg_ref, sgt_ref), 3)
    yts = [
        sketch_of_pair(grams[2 * n], pairs[:, 64 * n : 64 * n + 64], grams[2 * n + 1], signs_t)
        for n in range(2)
    ]
    bs, moments = compress(yts, signs)
    cross = mm_nt(mm(bs[0], inside), bs[1])
    first, second = (gram_of(u, m) for u, m in zip(bs, moments))
    signs, signs_t = signs_of((sg_ref, sgt_ref), 4)
    (b,), _ = compress([sketch_of_pair(first, cross, second, signs_t)], signs)
    lower = signs_mm(signs_t[:, :64], bs[0])
    upper = signs_mm(signs_t[:, 64:], bs[1])
    w = mm(b, jnp.concatenate([lower, upper], axis=1)) * (0.5**0.5)
    lane = lax.broadcasted_iota(jnp.int32, (128, 128), 1)
    block = lax.shift_right_logical(lane, 5)
    mine = jnp.zeros((128, 128), F32)
    for q in range(4):
        own = jnp.concatenate([s_ref[0, q], s_ref[1, q]], axis=0)
        turned = pltpu.roll(own, lax.rem(32 * q - 32 * place + 128, 128), 1)
        mine = jnp.where(block == q, turned, mine)
    out_ref[...] = product(w, mine)


def call(kernel, out_shapes, smem, *args, scratch=(), limit=16, cost=None):
    specs = [SMEM] * smem + [VMEM] * (len(args) - smem)
    return pl.pallas_call(
        kernel,
        out_shape=out_shapes,
        in_specs=specs,
        out_specs=jax.tree.map(lambda _: VMEM, out_shapes),
        scratch_shapes=list(scratch),
        cost_estimate=cost,
        compiler_params=pltpu.CompilerParams(vmem_limit_bytes=limit << 20),
    )(*args)


def in_hbm(value):
    return pltpu.with_memory_space_constraint(value, pltpu.HBM)


def shape(*dims):
    return jax.ShapeDtypeStruct(dims, F32)


def shift(value, axis, by):
    n = lax.axis_size(axis)
    return lax.ppermute(value, axis, [(i, (i + by) % n) for i in range(n)])


def from_ring(value, axis):
    return [value] + [shift(value, axis, d) for d in (1, 2, 3)]


def total(parts):
    return (parts[0] + parts[1]) + (parts[2] + parts[3])


def sum_over(value, axis):
    peers = lax.axis_size(axis)
    sent = jnp.broadcast_to(value[None], (peers, *value.shape))
    return lax.all_to_all(sent, axis, 0, 0, tiled=True).sum(axis=0)


def per_device(init_state, coef, source, amplitudes, sample_idx, step_counts, sketch_signs):
    field = init_state[0]
    rate = coef[0]
    slabs = ("z", "core")
    n = lax.axis_size(slabs)
    between = [(i, i + 1) for i in range(1, n - 1, 2)] + [(i, i - 1) for i in range(2, n, 2)]
    ends, cross, chip, amp = pl.pallas_call(
        pack_kernel,
        out_shape=(shape(2, 1040, 128), shape(1040, 128), shape(1040, 128), shape(128, 128)),
        in_specs=[pl.BlockSpec(memory_space=pltpu.HBM)] * 5,
        out_specs=(VMEM,) * 4,
        scratch_shapes=[
            pltpu.VMEM((2048, 128), F32),
            pltpu.SMEM((1, 128), jnp.int32),
            pltpu.SMEM((64,), F32),
            pltpu.SemaphoreType.DMA((10,)),
        ],
        compiler_params=pltpu.CompilerParams(vmem_limit_bytes=16 << 20),
    )(
        *(
            in_hbm(v)
            for v in (field.reshape(2048, 128), rate, source, sample_idx, amplitudes)
        )
    )
    bits = jnp.swapaxes(sketch_signs, 1, 2)
    cross = lax.ppermute(cross, slabs, between)
    chip = shift(chip, "core", 1)
    last, prev, first_signs = call(
        inner_kernel,
        (
            shape(16, 128, 128),
            shape(16, 128, 128),
            jax.ShapeDtypeStruct((64, 128), jnp.bfloat16),
        ),
        1,
        step_counts,
        ends,
        amp,
        bits,
        scratch=[pltpu.VMEM((128, 128), F32)] * 3 + [pltpu.VMEM((2, 128, 128), F32)],
        cost=pl.CostEstimate(flops=4_000_000_000, bytes_accessed=4_000_000, transcendentals=0),
    )
    final, sks, *chunks = call(
        flow_kernel,
        (shape(16, 128, 128), shape(16, 64, 128)) + (shape(4, 64, 128),) * 4,
        1,
        step_counts,
        last,
        prev,
        cross,
        chip,
        ends,
        amp,
        first_signs,
        scratch=[pltpu.VMEM((256, 128), F32)] * 3
        + [
            pltpu.VMEM((2, 256, 128), F32),
            pltpu.VMEM((4, 4, 64, 128), F32),
            pltpu.VMEM((2, 1040, 128), F32),
        ],
    )
    yt, signs, signs_t = call(
        leaf_sum_kernel,
        (
            shape(64, 128),
            jax.ShapeDtypeStruct((5, 128, 64), jnp.bfloat16),
            jax.ShapeDtypeStruct((5, 64, 128), jnp.bfloat16),
        ),
        0,
        final,
        sks,
        bits,
        cost=pl.CostEstimate(flops=2_000_000_000, bytes_accessed=2_000_000, transcendentals=0),
    )
    got = [chunks[0]] + [shift(chunks[d], "y", d) for d in (1, 2, 3)]
    keep, send, sketches = call(
        cross_kernel,
        (shape(128, 128), shape(128, 128), shape(4, 4, 64, 128)),
        0,
        yt,
        *got,
        scratch=[pltpu.VMEM((192, 128), F32), pltpu.VMEM((2, 128, 128), F32)],
    )
    half = keep + shift(send, "core", 1)
    quarters = [half[32:56]] + [shift(half[32 + 24 * d : 56 + 24 * d], "y", d) for d in (1, 2, 3)]
    own = sum_over(jnp.concatenate([half[:32], total(quarters)], axis=0), "z")
    leaf = call(leaf_kernel, shape(112, 128), 0, own, shift(own, "core", 1), signs, signs_t)
    piece = call(
        middle_kernel,
        shape(288, 128),
        0,
        *from_ring(leaf, "y"),
        sketches,
        signs,
        signs_t,
        scratch=[pltpu.VMEM((4, 112, 128), F32), pltpu.VMEM((192, 128), F32)],
    )
    pieces = from_ring(piece, "x")
    s, keep, send = call(
        upper_kernel,
        (shape(2, 4, 64, 128), shape(48, 128), shape(48, 128)),
        0,
        *pieces,
        signs,
        signs_t,
        scratch=[pltpu.VMEM((4, 256, 128), F32), pltpu.VMEM((2, 48, 128), F32)],
    )
    half = keep + shift(send, "core", 1)
    own = sum_over(total(from_ring(half, "y")), "z")
    out = call(
        last_kernel,
        shape(64, 128),
        0,
        own,
        shift(own, "core", 1),
        *pieces,
        s,
        signs,
        signs_t,
        scratch=[pltpu.VMEM((4, 32, 128), F32)],
    )
    return out.reshape(64, 16, 8)


def solution(mesh):
    fine = Mesh(mesh.devices.reshape(4, 4, 8, 2), ("x", "y", "z", "core"))
    group, slab = ("x", "y"), ("z", "core")
    return jax.shard_map(
        per_device,
        mesh=fine,
        in_specs=(
            P(group, None, slab, None),
            P(group, slab, None),
            P(slab, None),
            P(),
            P(group, None),
            P(group),
            P(),
        ),
        out_specs=P(None, slab, group),
        check_vma=False,
    )
```
